256 devices in a mesh: ctx: 32 (over z, y), head: 8 (over x, core).
Axes of the slice: x: 4, y: 4, z: 8, core: 2. Of those that a mesh axis runs over, the one named last changes fastest.
Arguments:
- queries: bfloat16 [16384, 5120], P('ctx', 'head'), may hold values from -34 to 34
- key_rows: bfloat16 [16384, 5120], P('ctx', 'head'), may hold values from -8 to 8
- value_rows: bfloat16 [16384, 5120], P('ctx', 'head'), may hold values from -23 to 23
- learning_rates: float32 [8, 16384], P('head', 'ctx'), may hold values from 0.02 to 1
- fast_gate: bfloat16 [8, 640, 640], P('head'), may hold values from -0.25 to 0.25
- fast_lift: bfloat16 [8, 640, 640], P('head'), may hold values from -0.25 to 0.25
- fast_down: bfloat16 [8, 640, 640], P('head'), may hold values from -0.25 to 0.25
- output_gain: float32 [5120], P('head'), may hold values from 0.25 to 1.75
- output_weight: bfloat16 [5120, 5120], P(None, 'head'), may hold values from -0.078125 to 0.078125
Outputs:
- layer_output: bfloat16 [16384, 5120], P('ctx', 'head')
The draws below stay inside these ranges and needn't reach their ends.
All inputs are finite; a program needn't handle non-finite values.
Results may differ from the reference program's by a relative error of at most 0.025.
Values may be sent and summed in bfloat16 or wider, within the bound.
A program may use at most 128 MiB of HBM per device.

```python
import math
import jax
import jax.numpy as jnp
from jax import lax

D = 5120
HEADS = 8
HD = 640
ATT_HD = 128
WINDOW = 512
NS_ITERS = 3
TOK_DEV = 512
GROUP = 16384


def feature_signs(key, count):
    return 2.0 * jax.random.bernoulli(key, 0.5, (count,)).astype(jnp.float32) - 1.0


def drawn_pair(key):
    base_key = jax.random.fold_in(key, 4111)
    first_key, second_key = jax.random.split(base_key)
    sign_key, level_key = jax.random.split(jax.random.fold_in(key, 5227))
    feature_count = HEADS * HD
    feature = jnp.arange(feature_count, dtype=jnp.int32) % HD
    spread = 0.6 * 3.0 ** (feature.astype(jnp.float32) / (HD - 1))
    shared = 0.4 * feature_signs(sign_key, feature_count) * jax.random.uniform(level_key, (feature_count,), jnp.float32, 0.5, 1.5)
    raw_keys = jnp.clip(jax.random.normal(first_key, (GROUP, feature_count), jnp.float32), -4.0, 4.0)
    raw_queries = jnp.clip(jax.random.normal(second_key, (GROUP, feature_count), jnp.float32), -4.0, 4.0)
    key_values = jnp.clip((raw_keys + shared[None, :]) * spread[None, :], -8.0, 8.0)
    query_values = raw_queries + (shared * spread)[None, :]
    return (query_values, key_values)


def draw_queries(key, part):
    query_values, key_values = drawn_pair(key)
    return query_values.astype(jnp.bfloat16)


def draw_key_rows(key, part):
    query_values, key_values = drawn_pair(key)
    return key_values.astype(jnp.bfloat16)


def draw_value_rows(key, part):
    base_key = jax.random.fold_in(key, 7307)
    sign_key, level_key, noise_key = jax.random.split(base_key, 3)
    feature_count = HEADS * HD
    shared = 0.35 * feature_signs(sign_key, feature_count) * jax.random.uniform(level_key, (feature_count,), jnp.float32, 0.5, 1.5)
    raw_values = jnp.clip(jax.random.normal(noise_key, (GROUP, feature_count), jnp.float32), -5.0, 5.0)
    return (4.0 * (raw_values + shared[None, :])).astype(jnp.bfloat16)


def steps_of(key, dims, shards, low, high):
    gain = 1.0
    for position, shards_of in shards:
        heights = jax.random.uniform(jax.random.fold_in(jax.random.fold_in(key, 6), position), (shards_of,), jnp.float32, low / len(shards), high / len(shards))
        gain = gain * jnp.repeat(jnp.exp(heights), dims[position] // shards_of).reshape((-1,) + (1,) * (len(dims) - 1 - position))
    return gain


def normal_values(own_key, extent, width, reach, cuts=(), held_as=jnp.bfloat16):
    level = steps_of(own_key, extent, cuts, -0.22, 0.18) if cuts else 1.0
    drawn = jax.random.normal(own_key, extent, jnp.float32) * width * level
    return jnp.minimum(jnp.maximum(drawn, -reach), reach).astype(held_as)


def setup_inputs(seed: int = 0) -> dict:
    key_of = jax.random.split(jax.random.key(seed), 10)
    queries = draw_queries(jax.random.fold_in(key_of[9], 71), 0)
    key_rows = draw_key_rows(jax.random.fold_in(key_of[9], 71), 0)
    value_rows = draw_value_rows(jax.random.fold_in(key_of[9], 71), 0)
    learning_rates = jnp.clip(jnp.exp(math.log(1.0) - 3.912023 * jax.random.uniform(key_of[3], (HEADS, GROUP), jnp.float32) ** steps_of(key_of[3], (HEADS, GROUP), ((0, 8), (1, 32)), -0.2, 0.2)), 0.02, 1.0)
    fast_gate = normal_values(key_of[4], (HEADS, HD, HD), HD ** -0.5, 0.25, ((0, 8),))
    fast_lift = normal_values(key_of[5], (HEADS, HD, HD), HD ** -0.5, 0.25, ((0, 8),))
    fast_down = normal_values(key_of[6], (HEADS, HD, HD), HD ** -0.5, 0.25, ((0, 8),))
    output_gain = jnp.clip(1.0 + 0.15 * jax.random.normal(key_of[7], (HEADS * HD,), jnp.float32), 0.25, 1.75)
    output_weight = normal_values(key_of[8], (HEADS * HD, D), (HEADS * HD) ** -0.5, 0.078125, ((1, 8),))
    return dict(queries=queries, key_rows=key_rows, value_rows=value_rows, learning_rates=learning_rates, fast_gate=fast_gate, fast_lift=fast_lift, fast_down=fast_down, output_gain=output_gain, output_weight=output_weight)


quintic_first = 3.4445
quintic_second = -4.775
quintic_third = 2.0315

def settle(values):
    return lax.optimization_barrier(values.astype(jnp.bfloat16))

def silu_slope(inputs):
    logistic = jax.nn.sigmoid(inputs)
    return logistic * (1.0 + inputs * (1.0 - logistic))

def window_attention(head_queries, head_keys, head_values):
    stride = min(512, TOK_DEV)
    blocks = GROUP // stride
    padding = jnp.zeros((WINDOW, ATT_HD), jnp.bfloat16)
    keys_padded = jnp.concatenate([padding, head_keys], axis=0)
    values_padded = jnp.concatenate([padding, head_values], axis=0)

    def one_block(number):
        first_row = number * stride
        query_block = lax.dynamic_slice_in_dim(head_queries, first_row, stride, 0)
        key_block = lax.dynamic_slice_in_dim(keys_padded, first_row, stride + WINDOW, 0)
        value_block = lax.dynamic_slice_in_dim(values_padded, first_row, stride + WINDOW, 0)
        scores = jnp.dot(query_block, key_block.T, preferred_element_type=jnp.float32) * ATT_HD ** (-0.5)
        query_place = first_row + jnp.arange(stride, dtype=jnp.int32)[:, None]
        key_place = first_row - WINDOW + jnp.arange(stride + WINDOW, dtype=jnp.int32)[None, :]
        allowed = (key_place > query_place - WINDOW) & (key_place <= query_place) & (key_place >= 0)
        scores = jnp.where(allowed, scores, -1e+30)
        row_peak = lax.optimization_barrier(jnp.max(scores, axis=1, keepdims=True))
        weights = jnp.exp(scores - row_peak)
        row_total = lax.optimization_barrier(jnp.sum(weights, axis=1, keepdims=True))
        probabilities = (weights / row_total).astype(jnp.bfloat16)
        return jnp.dot(probabilities, value_block, preferred_element_type=jnp.float32)
    attended = lax.map(one_block, jnp.arange(blocks, dtype=jnp.int32))
    return attended.reshape(GROUP, ATT_HD)

def orthogonalize(gradients):
    squares = lax.optimization_barrier(jnp.sum(gradients * gradients, axis=(1, 2), keepdims=True))
    current = settle(gradients / (jnp.sqrt(squares) + 1e-06))
    for iteration in range(NS_ITERS):
        widened = current.astype(jnp.float32)
        gram_full = settle(jnp.einsum('mrd,med->mre', widened, widened, precision=lax.Precision.HIGHEST))
        product = settle(jnp.einsum('mre,med->mrd', gram_full.astype(jnp.float32), widened, precision=lax.Precision.HIGHEST))
        second = jnp.einsum('mre,med->mrd', gram_full.astype(jnp.float32), product.astype(jnp.float32), precision=lax.Precision.HIGHEST)
        current = settle(quintic_first * widened + quintic_second * product.astype(jnp.float32) + quintic_third * second)
    return current

def head_output(head_queries, head_keys, head_values, head_rates, gate_init, lift_init, down_init, head_gain):
    gate_pre = jnp.dot(head_keys, gate_init, preferred_element_type=jnp.float32)
    lift_pre = jnp.dot(head_keys, lift_init, preferred_element_type=jnp.float32)
    hidden = (jax.nn.silu(gate_pre) * lift_pre).astype(jnp.bfloat16)
    scaled = (head_rates[:, None] * head_values.astype(jnp.float32)).astype(jnp.bfloat16)
    backward = jnp.dot(scaled, down_init.T, preferred_element_type=jnp.float32)
    grad_gate = (backward * lift_pre * silu_slope(gate_pre)).astype(jnp.bfloat16)
    grad_lift = (backward * jax.nn.silu(gate_pre)).astype(jnp.bfloat16)
    gradients = jnp.stack([jnp.dot(head_keys.T, grad_gate, preferred_element_type=jnp.float32), jnp.dot(head_keys.T, grad_lift, preferred_element_type=jnp.float32), jnp.dot(hidden.T, scaled, preferred_element_type=jnp.float32)])
    directions = orthogonalize(gradients)
    initial = jnp.stack([gate_init, lift_init, down_init]).astype(jnp.float32)
    updated = initial + directions.astype(jnp.float32)
    target = jnp.sqrt(lax.optimization_barrier(jnp.sum(initial * initial, axis=1, keepdims=True)))
    current = jnp.sqrt(lax.optimization_barrier(jnp.sum(updated * updated, axis=1, keepdims=True)) + 1e-06)
    renewed = (updated * (target / current)).astype(jnp.bfloat16)
    applied_gate = jnp.dot(head_queries, renewed[0], preferred_element_type=jnp.float32)
    applied_lift = jnp.dot(head_queries, renewed[1], preferred_element_type=jnp.float32)
    applied_hidden = (jax.nn.silu(applied_gate) * applied_lift).astype(jnp.bfloat16)
    fast_result = jnp.dot(applied_hidden, renewed[2], preferred_element_type=jnp.float32)
    scale_back = lax.rsqrt(lax.optimization_barrier(jnp.mean(fast_result * fast_result, axis=1, keepdims=True)) + 1e-06)
    return fast_result * scale_back * head_gain[None, :]

def reference(queries, key_rows, value_rows, learning_rates, fast_gate, fast_lift, fast_down, output_gain, output_weight):
    pieces = []
    for head_number in range(HEADS):
        low = head_number * HD
        head_queries = queries[:, low:low + HD]
        head_keys = key_rows[:, low:low + HD]
        head_values = value_rows[:, low:low + HD]
        attended_parts = []
        for inner in range(HD // ATT_HD):
            start = inner * ATT_HD
            attended_parts.append(window_attention(head_queries[:, start:start + ATT_HD], head_keys[:, start:start + ATT_HD], head_values[:, start:start + ATT_HD]))
        attended = jnp.concatenate(attended_parts, axis=1)
        fast_part = head_output(head_queries, head_keys, head_values, learning_rates[head_number], fast_gate[head_number], fast_lift[head_number], fast_down[head_number], output_gain[low:low + HD])
        pieces.append((attended + fast_part).astype(jnp.bfloat16))
    combined = jnp.concatenate(pieces, axis=1)
    return jnp.dot(combined, output_weight, preferred_element_type=jnp.float32).astype(jnp.bfloat16)
```

```python
import jax
import jax.numpy as jnp
from jax import lax
from jax.sharding import PartitionSpec as P

HD = 640
ATT_HD = 128
WINDOW = 512
NS_ITERS = 3


quintic_first = 3.4445
quintic_second = -4.775
quintic_third = 2.0315


def shifted(array, axis, by):
    size = lax.axis_size(axis)
    pairs = [(i, i + by) for i in range(size) if 0 <= i + by < size]
    return lax.ppermute(array, axis, pairs)


def settle(values):
    return lax.optimization_barrier(values.astype(jnp.bfloat16))


def silu_slope(inputs):
    logistic = jax.nn.sigmoid(inputs)
    return logistic * (1.0 + inputs * (1.0 - logistic))


def local_attention(queries, key_rows, value_rows, earlier_keys, earlier_values, device_row):
    tokens = queries.shape[0]
    heads_here = queries.shape[1] // ATT_HD
    stride = min(512, tokens)
    keys_joined = jnp.concatenate([earlier_keys, key_rows], axis=0)
    values_joined = jnp.concatenate([earlier_values, value_rows], axis=0)
    query_block = queries.reshape(stride, heads_here, ATT_HD)
    key_block = keys_joined.reshape(stride + WINDOW, heads_here, ATT_HD)
    value_block = values_joined.reshape(stride + WINDOW, heads_here, ATT_HD)
    scores = jnp.einsum(
        "qhd,khd->hqk", query_block, key_block, preferred_element_type=jnp.float32
    ) * ATT_HD ** (-0.5)
    query_place = device_row + 0 + jnp.arange(stride, dtype=jnp.int32)[:, None]
    key_place = device_row + 0 - WINDOW + jnp.arange(stride + WINDOW, dtype=jnp.int32)[None, :]
    allowed = (key_place > query_place - WINDOW) & (key_place <= query_place) & (key_place >= 0)
    scores = jnp.where(allowed[None], scores, -1e30)
    row_peak = jnp.max(scores, axis=2, keepdims=True)
    weights = jnp.exp(scores - row_peak)
    row_total = jnp.sum(weights, axis=2, keepdims=True)
    probabilities = (weights / row_total).astype(jnp.bfloat16)
    block_out = jnp.einsum(
        "hqk,khd->qhd", probabilities, value_block, preferred_element_type=jnp.float32
    )
    outputs = block_out.reshape(stride, heads_here * ATT_HD)
    return outputs


def on_device(
    queries,
    key_rows,
    value_rows,
    learning_rates,
    fast_gate,
    fast_lift,
    fast_down,
    output_gain,
    output_weight,
):
    tokens = queries.shape[0]
    heads_here = queries.shape[1] // HD
    device_row = lax.axis_index("ctx") * tokens
    earlier_keys, earlier_values = shifted((key_rows, value_rows), "ctx", 1)
    attended = local_attention(
        queries, key_rows, value_rows, earlier_keys, earlier_values, device_row
    )
    attended = attended.reshape(tokens, heads_here, HD)
    key_heads = key_rows.reshape(tokens, heads_here, HD)
    gate_pre = jnp.einsum("thd,hde->the", key_heads, fast_gate, preferred_element_type=jnp.float32)
    lift_pre = jnp.einsum("thd,hde->the", key_heads, fast_lift, preferred_element_type=jnp.float32)
    hidden = (jax.nn.silu(gate_pre) * lift_pre).astype(jnp.bfloat16)
    token_rates = jnp.transpose(learning_rates)
    scaled = (
        token_rates[:, :, None] * value_rows.reshape(tokens, heads_here, HD).astype(jnp.float32)
    ).astype(jnp.bfloat16)
    backward = jnp.einsum("thd,hed->the", scaled, fast_down, preferred_element_type=jnp.float32)
    grad_gate = (backward * lift_pre * silu_slope(gate_pre)).astype(jnp.bfloat16)
    grad_lift = (backward * jax.nn.silu(gate_pre)).astype(jnp.bfloat16)
    partial_gate = jnp.einsum(
        "thd,the->hde", key_heads, grad_gate, preferred_element_type=jnp.float32
    )
    partial_lift = jnp.einsum(
        "thd,the->hde", key_heads, grad_lift, preferred_element_type=jnp.float32
    )
    partial_down = jnp.einsum("the,thd->hed", hidden, scaled, preferred_element_type=jnp.float32)
    partials = jnp.stack([partial_gate, partial_lift, partial_down], axis=1).reshape(
        3 * heads_here, HD, HD
    )
    summed = lax.psum(partials.astype(jnp.bfloat16), "ctx").astype(jnp.float32)
    squares = jnp.sum(summed * summed, axis=(1, 2))
    iterate_full = settle(summed / (jnp.sqrt(squares)[:, None, None] + 1e-06))
    for iteration in range(NS_ITERS):
        gram = settle(
            jnp.einsum(
                "mrd,med->mre", iterate_full, iterate_full, preferred_element_type=jnp.float32
            )
        )
        product = settle(
            jnp.einsum("mre,med->mrd", gram, iterate_full, preferred_element_type=jnp.float32)
        )
        second = jnp.einsum("mre,med->mrd", gram, product, preferred_element_type=jnp.float32)
        iterate_full = settle(
            quintic_first * iterate_full.astype(jnp.float32)
            + quintic_second * product.astype(jnp.float32)
            + quintic_third * second
        )
    initial = (
        jnp.stack([fast_gate, fast_lift, fast_down], axis=1)
        .reshape(3 * heads_here, HD, HD)
        .astype(jnp.float32)
    )
    updated = initial + iterate_full.astype(jnp.float32)
    target = jnp.sqrt(jnp.sum(initial * initial, axis=1, keepdims=True))
    current = jnp.sqrt(jnp.sum(updated * updated, axis=1, keepdims=True) + 1e-06)
    renewed = (updated * (target / current)).astype(jnp.bfloat16).reshape(heads_here, 3, HD, HD)
    query_heads = queries.reshape(tokens, heads_here, HD)
    applied_gate = jnp.einsum(
        "thd,hde->the", query_heads, renewed[:, 0], preferred_element_type=jnp.float32
    )
    applied_lift = jnp.einsum(
        "thd,hde->the", query_heads, renewed[:, 1], preferred_element_type=jnp.float32
    )
    applied_hidden = (jax.nn.silu(applied_gate) * applied_lift).astype(jnp.bfloat16)
    fast_result = jnp.einsum(
        "the,hed->thd", applied_hidden, renewed[:, 2], preferred_element_type=jnp.float32
    )
    scale_back = lax.rsqrt(jnp.mean(fast_result * fast_result, axis=2, keepdims=True) + 1e-06)
    normed = fast_result * scale_back * output_gain.reshape(heads_here, HD)[None]
    combined = (attended + normed).astype(jnp.bfloat16).reshape(tokens, heads_here * HD)
    projected = jnp.dot(
        lax.all_gather(combined, "head", axis=1, tiled=True),
        output_weight,
        preferred_element_type=jnp.float32,
    )
    return projected.astype(jnp.bfloat16)


def solution(mesh):
    return jax.shard_map(
        on_device,
        mesh=mesh,
        in_specs=(
            P("ctx", "head"),
            P("ctx", "head"),
            P("ctx", "head"),
            P("head", "ctx"),
            P("head", None, None),
            P("head", None, None),
            P("head", None, None),
            P("head"),
            P(None, "head"),
        ),
        out_specs=P("ctx", "head"),
        check_vma=False,
    )
```

```python
import jax
import jax.numpy as jnp
from jax import lax
from jax.experimental import pallas as pl
from jax.experimental.pallas import tpu as pltpu
from jax.sharding import PartitionSpec as P

HD = 640
ATT_HD = 128
NS_ITERS = 3
TOK = 512
NZ, NY, NX = 8, 4, 4
ROWS = HD // NZ
TOP = 48
TILE = 128
MESH = pl.DeviceIdType.MESH
BF16 = jnp.bfloat16
F32 = jnp.float32

quintic_first = 3.4445
quintic_second = -4.775
quintic_third = 2.0315


def dot(a, b, ca=1, cb=0):
    return lax.dot_general(a, b, (((ca,), (cb,)), ((), ())), preferred_element_type=F32)


def logistic(x):
    return 1.0 / (1.0 + jnp.exp(-x))


def remote(src, dst, send_sem, recv_sem, device):
    return pltpu.make_async_remote_copy(
        src_ref=src, dst_ref=dst, send_sem=send_sem, recv_sem=recv_sem,
        device_id=device, device_id_type=MESH,
    )


def gradient_rows(rows, k, v, rates, wg, wl, wd, hid, scaled, g_gate, g_lift):
    keys = k[rows, :]
    gate_pre = dot(keys, wg[...])
    lift_pre = dot(keys, wl[...])
    sig = logistic(gate_pre)
    silu = gate_pre * sig
    hid[rows, :] = (silu * lift_pre).astype(BF16)
    sc = (rates[rows, :] * v[rows, :].astype(F32)).astype(BF16)
    scaled[rows, :] = sc
    backward = dot(sc, wd[...], 1, 1)
    g_gate[rows, :] = (backward * lift_pre * (sig * (1.0 + gate_pre * (1.0 - sig)))).astype(BF16)
    g_lift[rows, :] = (backward * silu).astype(BF16)


def update_kernel(
    q, k, v, rates, wg, wl, wd,
    att, ren,
    part, rbuf, ybuf, full, kh, vh, pbuf, hid, scaled, g_gate, g_lift, gram, prod, x_it,
    halo_s, halo_r, rs_s, rs_r, y_s, y_r, ag_s, ag_r,
):
    ctx = lax.axis_index("ctx")
    z, y = ctx // NY, ctx % NY
    up = {"ctx": ((z + 1) % NZ) * NY + y}
    down = {"ctx": ((z + NZ - 1) % NZ) * NY + y}
    peers = [{"ctx": z * NY + (y + d) % NY} for d in (1, 2, 3)]
    after = {"ctx": (ctx + 1) % (NZ * NY)}
    before = {"ctx": (ctx + NZ * NY - 1) % (NZ * NY)}
    started = []

    def go(*args):
        copy = remote(*args)
        copy.start()
        started.append(copy)
        return copy

    barrier = pltpu.get_barrier_semaphore()
    everyone = [up, down, after, before] + peers
    for device in everyone:
        pl.semaphore_signal(barrier, inc=1, device_id=device, device_id_type=MESH)
    pl.semaphore_wait(barrier, len(everyone))

    halo_k = go(k, kh, halo_s.at[0], halo_r.at[0], after)
    halo_v = go(v, vh, halo_s.at[1], halo_r.at[1], after)

    @pl.loop(0, TOK // 256)
    def _(i):
        rows = pl.ds(pl.multiple_of(i * 256, 256), 256)
        gradient_rows(rows, k, v, rates, wg, wl, wd, hid, scaled, g_gate, g_lift)

    def block(c, low=0, size=ROWS):
        return pl.ds(pl.multiple_of(((c + 2 * NZ) % NZ) * ROWS + low, 16), size)

    def rs_begin(s):
        go(part.at[s, block(z + 4, 0, TOP)], rbuf.at[s, 0, 0, pl.ds(0, TOP)],
           rs_s.at[s, 0, 0], rs_r.at[s, 0, 0], up)
        go(part.at[s, block(z + 4, TOP, ROWS - TOP)], rbuf.at[s, 1, 0, pl.ds(TOP, ROWS - TOP)],
           rs_s.at[s, 1, 0], rs_r.at[s, 1, 0], down)

    def rs_arrived(s, d, step):
        if step == 1:
            where = rbuf.at[s, d, 0, pl.ds(0, TOP) if d == 0 else pl.ds(TOP, ROWS - TOP)]
        else:
            where = rbuf.at[s, d, step - 1]
        remote(where, where, rs_s.at[s, d, step - 1], rs_r.at[s, d, step - 1],
               up if d == 0 else down).wait_recv()

    def rs_step(s, step):
        for d in (0, 1):
            rs_arrived(s, d, step)
            c = z + 4 - step if d == 0 else z - 4 + step
            spot = rbuf.at[s, d, step - 1]
            if step == 1:
                lo, size = (0, TOP) if d == 0 else (TOP, ROWS - TOP)
                olo, osize = (TOP, ROWS - TOP) if d == 0 else (0, TOP)
                spot[pl.ds(lo, size), :] = (
                    spot[pl.ds(lo, size), :].astype(F32) + part[s, block(c, lo, size), :].astype(F32)
                ).astype(BF16)
                spot[pl.ds(olo, osize), :] = part[s, block(c, olo, osize), :]
            else:
                spot[...] = (spot[...].astype(F32) + part[s, block(c), :].astype(F32)).astype(BF16)
            go(spot, rbuf.at[s, d, step], rs_s.at[s, d, step], rs_r.at[s, d, step],
               up if d == 0 else down)

    def rs_end(s):
        rs_arrived(s, 0, 4)
        rs_arrived(s, 1, 4)
        ybuf[s, y] = (
            part[s, block(z), :].astype(F32) + rbuf[s, 0, 3].astype(F32) + rbuf[s, 1, 3].astype(F32)
        ).astype(BF16)
        for d in range(3):
            go(ybuf.at[s, y], ybuf.at[s, y], y_s.at[s, d], y_r.at[s, d], peers[d])

    def ag_begin(s):
        for d in range(3):
            spot = ybuf.at[s, (y + 3 - d) % NY]
            remote(spot, spot, y_s.at[s, d], y_r.at[s, d], peers[d]).wait_recv()
        total = ybuf[s, 0].astype(F32) + ybuf[s, 1].astype(F32)
        total += ybuf[s, 2].astype(F32) + ybuf[s, 3].astype(F32)
        full[s, block(z), :] = total.astype(BF16)
        spot = full.at[s, block(z)]
        go(spot, spot, ag_s.at[s, 0, 0], ag_r.at[s, 0, 0], up)
        go(spot, spot, ag_s.at[s, 1, 0], ag_r.at[s, 1, 0], down)

    def ag_step(s, step):
        for d in (0, 1):
            c = z - step if d == 0 else z + step
            part_rows = (0, TOP) if d == 0 else (TOP, ROWS - TOP)
            lo, size = part_rows if step == 4 else (0, ROWS)
            spot = full.at[s, block(c, lo, size)]
            remote(spot, spot, ag_s.at[s, d, step - 1], ag_r.at[s, d, step - 1],
                   up if d == 0 else down).wait_recv()
            if step < 4:
                lo, size = part_rows if step == 3 else (0, ROWS)
                spot = full.at[s, block(c, lo, size)]
                go(spot, spot, ag_s.at[s, d, step], ag_r.at[s, d, step], up if d == 0 else down)

    def weights_of(h):
        cols = pl.ds(h * ATT_HD, ATT_HD)
        scale = ATT_HD ** (-0.5)

        @pl.loop(0, TOK // TILE)
        def _(i):
            rows = pl.ds(pl.multiple_of(i * TILE, TILE), TILE)
            own = dot(q[rows, cols], k[:, cols], 1, 1)
            old = dot(q[rows, cols], kh[:, cols], 1, 1)
            row = i * TILE + lax.broadcasted_iota(jnp.int32, (TILE, TOK), 0)
            col = lax.broadcasted_iota(jnp.int32, (TILE, TOK), 1)
            first = jnp.where(ctx == 0, -1e30, 0.0).astype(F32)
            scores = jnp.where(col <= row, own * scale, old * scale + first)
            peak = jnp.max(scores, axis=1, keepdims=True)
            w = jnp.exp(scores - peak)
            total = jnp.sum(w, axis=1, keepdims=True)
            pbuf[h, rows, :] = (w / total).astype(BF16)

    def attend(h):
        cols = pl.ds(h * ATT_HD, ATT_HD)

        @pl.loop(0, TOK // TILE)
        def _(i):
            rows = pl.ds(pl.multiple_of(i * TILE, TILE), TILE)
            w = pbuf[h, rows, :]
            row = i * TILE + lax.broadcasted_iota(jnp.int32, (TILE, TOK), 0)
            col = lax.broadcasted_iota(jnp.int32, (TILE, TOK), 1)
            w_own = jnp.where(col <= row, w, jnp.zeros_like(w))
            w_old = jnp.where(col <= row, jnp.zeros_like(w), w)
            att[rows, cols] = dot(w_own, v[:, cols]) + dot(w_old, vh[:, cols])

    def orthogonalize(s):
        g = full[s].astype(F32)
        size = jnp.sqrt(jnp.sum(jnp.sum(g * g, axis=1, keepdims=True), axis=0, keepdims=True))
        x_it[...] = (g * (1.0 / (size + 1e-06))).astype(BF16)

        @pl.loop(0, NS_ITERS)
        def _(i):
            gram[...] = dot(x_it[...], x_it[...], 1, 1).astype(BF16)
            prod[...] = dot(gram[...], x_it[...]).astype(BF16)
            second = dot(gram[...], prod[...])
            x_it[...] = (
                quintic_first * x_it[...].astype(F32)
                + quintic_second * prod[...].astype(F32)
                + quintic_third * second
            ).astype(BF16)

        initial = (wd, wl, wg)[s][...].astype(F32)
        updated = initial + x_it[...].astype(F32)
        target = jnp.sqrt(jnp.sum(initial * initial, axis=0, keepdims=True))
        current = jnp.sqrt(jnp.sum(updated * updated, axis=0, keepdims=True) + 1e-06)
        ren[s] = (updated * (target / current)).astype(BF16)

    for s, (left, right) in enumerate(((hid, scaled), (k, g_lift), (k, g_gate))):
        part[s] = dot(left[...], right[...], 0, 0).astype(BF16)
        rs_begin(s)
    for step in (1, 2, 3):
        for s in range(3):
            rs_step(s, step)
    halo_k.wait_recv()
    for s in range(3):
        weights_of(s)
        rs_end(s)
    weights_of(3)
    ag_begin(0)
    weights_of(4)
    ag_begin(1)
    ag_begin(2)
    halo_v.wait_recv()
    for step in (1, 2, 3, 4):
        for s in range(3):
            ag_step(s, step)
        attend(step - 1)
    attend(4)
    for s in range(3):
        orthogonalize(s)
    for copy in started:
        copy.wait_send()


def update(queries, key_rows, value_rows, rates, fast_gate, fast_lift, fast_down):
    vmem = pl.BlockSpec(memory_space=pltpu.VMEM)
    dma = pltpu.SemaphoreType.DMA
    square = (HD, HD)
    tokens = (TOK, HD)
    return pl.pallas_call(
        update_kernel,
        name="fast_update",
        out_shape=(jax.ShapeDtypeStruct(tokens, F32), jax.ShapeDtypeStruct((3, HD, HD), BF16)),
        in_specs=[vmem] * 7,
        out_specs=(vmem, vmem),
        scratch_shapes=[
            pltpu.VMEM((3, HD, HD), BF16),
            pltpu.VMEM((3, 2, 4, ROWS, HD), BF16),
            pltpu.VMEM((3, NY, ROWS, HD), BF16),
            pltpu.VMEM((3, HD, HD), BF16),
            pltpu.VMEM(tokens, BF16),
            pltpu.VMEM(tokens, BF16),
            pltpu.VMEM((HD // ATT_HD, TOK, TOK), BF16),
            pltpu.VMEM(tokens, BF16),
            pltpu.VMEM(tokens, BF16),
            pltpu.VMEM(tokens, BF16),
            pltpu.VMEM(tokens, BF16),
            pltpu.VMEM(square, BF16),
            pltpu.VMEM(square, BF16),
            pltpu.VMEM(square, BF16),
            dma((2,)), dma((2,)),
            dma((3, 2, 4)), dma((3, 2, 4)),
            dma((3, 3)), dma((3, 3)),
            dma((3, 2, 4)), dma((3, 2, 4)),
        ],
        compiler_params=pltpu.CompilerParams(
            collective_id=0, has_side_effects=True, vmem_limit_bytes=60 * 1024 * 1024
        ),
    )(queries, key_rows, value_rows, rates, fast_gate, fast_lift, fast_down)


def project_kernel(
    q, att, ren, gain, weight, out,
    cbuf, wbuf, acc, w_sem, d1_s, d1_r, d2_s, d2_r, pr_s, pr_r,
):
    head = lax.axis_index("head")
    x, core = head // 2, head % 2

    def place(offset, other=0):
        side = (core + other) % 2
        return ((x + offset + NX) % NX) * 2 + side

    right, left, partner = ({"head": place(1)}, {"head": place(-1)}, {"head": place(0, 1)})
    started = []

    def go(*args):
        copy = remote(*args)
        copy.start()
        started.append(copy)

    def arrived(spot, send_sem, recv_sem, device):
        remote(spot, spot, send_sem, recv_sem, device).wait_recv()

    order = [place(0), place(0, 1), place(-1), place(1), place(-1, 1), place(1, 1), place(2), place(2, 1)]
    loads = [pltpu.make_async_copy(weight.at[h], wbuf.at[h], w_sem.at[i]) for i, h in enumerate(order)]
    for load in loads:
        load.start()

    barrier = pltpu.get_barrier_semaphore()
    for device in (right, left, partner):
        pl.semaphore_signal(barrier, inc=1, device_id=device, device_id_type=MESH)
    pl.semaphore_wait(barrier, 3)

    def rows_of(t, low=0, size=TILE):
        return pl.ds(t * TILE + low, size)

    chunks = TOK // TILE
    half = TILE // 2
    for t in range(chunks):
        rows = rows_of(t)
        gate = dot(q[rows, :], ren[2])
        lift = dot(q[rows, :], ren[1])
        applied = (gate * logistic(gate) * lift).astype(BF16)
        result = dot(applied, ren[0])
        back = lax.rsqrt(jnp.mean(result * result, axis=1, keepdims=True) + 1e-06)
        cbuf[head, rows, :] = (att[rows, :] + result * back * gain[...]).astype(BF16)
        spot = cbuf.at[head, rows]
        go(spot, spot, d1_s.at[0, t], d1_r.at[0, t], right)
        go(spot, spot, d1_s.at[1, t], d1_r.at[1, t], left)
        go(spot, spot, pr_s.at[0, t], pr_r.at[0, t], partner)

    def add(i, rows, first=False, last=False):
        h = order[i]
        value = dot(cbuf[h, rows, :], wbuf[h])
        if not first:
            value += acc[rows, :]
        if last:
            out[rows, :] = value.astype(BF16)
        else:
            acc[rows, :] = value

    whole = pl.ds(0, TOK)

    def near(t):
        for d in (0, 1):
            h = place(-1) if d == 0 else place(1)
            spot = cbuf.at[h, rows_of(t)]
            arrived(spot, d1_s.at[d, t], d1_r.at[d, t], left if d == 0 else right)
            piece = cbuf.at[h, rows_of(t, d * half, half)]
            go(piece, piece, d2_s.at[d, t], d2_r.at[d, t], right if d == 0 else left)
            go(spot, spot, pr_s.at[1 + d, t], pr_r.at[1 + d, t], partner)

    def far(t):
        h = place(2)
        for d in (0, 1):
            piece = cbuf.at[h, rows_of(t, d * half, half)]
            arrived(piece, d2_s.at[d, t], d2_r.at[d, t], left if d == 0 else right)
        spot = cbuf.at[h, rows_of(t)]
        go(spot, spot, pr_s.at[3, t], pr_r.at[3, t], partner)

    def mirrored(j, t):
        h = place((0, -1, 1, 2)[j], 1)
        spot = cbuf.at[h, rows_of(t)]
        arrived(spot, pr_s.at[j, t], pr_r.at[j, t], partner)

    near(0)
    loads[0].wait()
    add(0, whole, first=True)
    near(1)
    for t in range(chunks):
        mirrored(0, t)
    loads[1].wait()
    add(1, whole)
    near(2)
    near(3)
    far(0)
    loads[2].wait()
    add(2, whole)
    far(1)
    loads[3].wait()
    add(3, whole)
    for t in range(chunks):
        mirrored(1, t)
    loads[4].wait()
    add(4, whole)
    far(2)
    for t in range(chunks):
        mirrored(2, t)
    loads[5].wait()
    add(5, whole)
    loads[6].wait()
    add(6, pl.ds(0, 3 * TILE))
    for t in range(chunks - 1):
        mirrored(3, t)
    loads[7].wait()
    add(7, pl.ds(0, 3 * TILE), last=True)
    far(3)
    add(6, rows_of(3))
    mirrored(3, 3)
    add(7, rows_of(3), last=True)
    for copy in started:
        copy.wait_send()


def project(queries, attended, renewed, gain, weight):
    vmem = pl.BlockSpec(memory_space=pltpu.VMEM)
    dma = pltpu.SemaphoreType.DMA
    heads = 2 * NX
    chunks = TOK // TILE
    return pl.pallas_call(
        project_kernel,
        name="project",
        out_shape=jax.ShapeDtypeStruct((TOK, HD), BF16),
        in_specs=[vmem] * 4 + [pl.BlockSpec(memory_space=pl.ANY)],
        out_specs=vmem,
        scratch_shapes=[
            pltpu.VMEM((heads, TOK, HD), BF16),
            pltpu.VMEM((heads, HD, HD), BF16),
            pltpu.VMEM((TOK, HD), F32),
            dma((heads,)),
            dma((2, chunks)), dma((2, chunks)),
            dma((2, chunks)), dma((2, chunks)),
            dma((4, chunks)), dma((4, chunks)),
        ],
        compiler_params=pltpu.CompilerParams(
            collective_id=1, has_side_effects=True, vmem_limit_bytes=60 * 1024 * 1024
        ),
    )(queries, attended, renewed, gain, weight)


def on_device(
    queries, key_rows, value_rows, learning_rates, fast_gate, fast_lift, fast_down, output_gain, output_weight
):
    attended, renewed = update(
        queries, key_rows, value_rows, jnp.transpose(learning_rates), fast_gate[0], fast_lift[0], fast_down[0]
    )
    return project(
        queries, attended, renewed, output_gain[None], output_weight.reshape(2 * NX, HD, HD)
    )


def solution(mesh):
    return jax.shard_map(
        on_device,
        mesh=mesh,
        in_specs=(
            P("ctx", "head"),
            P("ctx", "head"),
            P("ctx", "head"),
            P("head", "ctx"),
            P("head", None, None),
            P("head", None, None),
            P("head", None, None),
            P("head"),
            P(None, "head"),
        ),
        out_specs=P("ctx", "head"),
        check_vma=False,
    )
```

```python
import math

import jax
import jax.numpy as jnp
from jax import lax
from jax.experimental import pallas as pl
from jax.experimental.pallas import tpu as pltpu
from jax.sharding import PartitionSpec as P

HD = 640
ATT_HD = 128
NS_ITERS = 3
TOK = 512
NZ, NY, NX = 8, 4, 4
ROWS = HD // NZ
TOP = 48
TILE = 128
MESH = pl.DeviceIdType.MESH
BF16 = jnp.bfloat16
F32 = jnp.float32

EXP_SCALE = ATT_HD ** (-0.5) * math.log2(math.e)

quintic_first = 3.4445
quintic_second = -4.775
quintic_third = 2.0315


def dot(a, b, ca=1, cb=0):
    return lax.dot_general(a, b, (((ca,), (cb,)), ((), ())), preferred_element_type=F32)


def logistic(x):
    return 1.0 / (1.0 + jnp.exp(-x))


def remote(src, dst, send_sem, recv_sem, device):
    return pltpu.make_async_remote_copy(
        src_ref=src, dst_ref=dst, send_sem=send_sem, recv_sem=recv_sem,
        device_id=device, device_id_type=MESH,
    )


def gradient_rows(rows, k, v, rates, wg, wl, wd, hid, scaled, g_gate, g_lift):
    keys = k[rows, :]
    gate_pre = dot(keys, wg[...])
    lift_pre = dot(keys, wl[...])
    sig = logistic(gate_pre)
    silu = gate_pre * sig
    hid[rows, :] = (silu * lift_pre).astype(BF16)
    sc = (rates[rows, :1] * v[rows, :].astype(F32)).astype(BF16)
    scaled[rows, :] = sc
    backward = dot(sc, wd[...], 1, 1)
    g_gate[rows, :] = (backward * lift_pre * (sig * (1.0 + gate_pre * (1.0 - sig)))).astype(BF16)
    g_lift[rows, :] = (backward * silu).astype(BF16)


def layer_kernel(
    q, k, v, rates, wg, wl, wd, gain, weight,
    out,
    part, rbuf, ybuf, full, kh, vh, relay, pbuf, hid, scaled, g_gate, g_lift, gram, prod, x_it,
    rate_col, att, ren, cbuf, wbuf, acc,
    halo_s, halo_r, x_s, x_r, rs_s, rs_r, y_s, y_r, ag_s, ag_r,
    w_sem, d1_s, d1_r, d2_s, d2_r, pr_s, pr_r,
):
    ctx = lax.axis_index("ctx")
    z, y = ctx // NY, ctx % NY
    up = {"ctx": ((z + 1) % NZ) * NY + y}
    down = {"ctx": ((z + NZ - 1) % NZ) * NY + y}
    peers = [{"ctx": z * NY + (y + d) % NY} for d in (1, 2, 3)]
    after = {"ctx": z * NY + (y + 1) % NY}
    head = lax.axis_index("head")
    x, core = head // 2, head % 2

    def place(offset, other=0):
        side = (core + other) % 2
        return ((x + offset + NX) % NX) * 2 + side

    right, left, partner = ({"head": place(1)}, {"head": place(-1)}, {"head": place(0, 1)})
    started = []

    def go(*args):
        copy = remote(*args)
        copy.start()
        started.append(copy)
        return copy

    def arrived(spot, send_sem, recv_sem, device):
        remote(spot, spot, send_sem, recv_sem, device).wait_recv()

    order = [place(0), place(0, 1), place(-1), place(1), place(-1, 1), place(1, 1), place(2), place(2, 1)]
    loads = [pltpu.make_async_copy(weight.at[h], wbuf.at[h], w_sem.at[i]) for i, h in enumerate(order)]
    for load in loads:
        load.start()

    barrier = pltpu.get_barrier_semaphore()
    everyone = [up, down, right, left, partner] + peers
    for device in everyone:
        pl.semaphore_signal(barrier, inc=1, device_id=device, device_id_type=MESH)
    pl.semaphore_wait(barrier, len(everyone))

    def piece(p):
        return pl.ds(p * TILE, TILE)

    def mine():
        return pl.ds(pl.multiple_of(y * TILE, TILE), TILE)

    def halo(i, half):
        source, target = ((k, kh), (v, vh))[i]
        rows = pl.ds(half * (TOK // 2), TOK // 2)
        return remote(source.at[rows], target.at[rows], halo_s.at[i, half], halo_r.at[i], after)

    def across(i, p):
        source = (k, v)[i]
        return remote(source.at[piece(p)], relay.at[i, 0], x_s.at[i, p], x_r.at[i, 0], {"ctx": z * NY + p})

    def climb(i, column):
        source, target = ((k, kh), (v, vh))[i]
        if column == 3:
            return remote(source.at[piece(3)], relay.at[i, 1], x_s.at[i, 3], x_r.at[i, 1], up)
        if column == 0:
            return remote(relay.at[i, 0], target.at[piece(0)], x_s.at[i, 3], halo_r.at[i], up)
        return remote(relay.at[i, 0], relay.at[i, 1], x_s.at[i, 3], x_r.at[i, 1], up)

    def land(i):
        target = (kh, vh)[i]
        return remote(relay.at[i, 1], target.at[mine()], x_s.at[i, 4], halo_r.at[i], {"ctx": z * NY})

    def halo_begin(i):
        @pl.when(y == 3)
        def _():
            for p in range(3):
                across(i, p).start()
            climb(i, 3).start()

    def halo_half(i, half):
        @pl.when(y != 3)
        def _():
            halo(i, half).start()

    def halo_climb(i):
        @pl.when(y != 3)
        def _():
            across(i, 0).wait_recv()

        @pl.when(y == 0)
        def _():
            climb(i, 0).start()

        @pl.when((y == 1) | (y == 2))
        def _():
            climb(i, 1).start()

    def halo_land(i):
        @pl.when(y != 0)
        def _():
            climb(i, 1).wait_recv()
            land(i).start()

    def halo_wait(i):
        target = (kh, vh)[i]
        remote(target, target, halo_s.at[i, 0], halo_r.at[i], after).wait_recv()

    def halo_sent(i):
        climb(i, 1).wait_send()

        @pl.when(y == 3)
        def _():
            for p in range(3):
                across(i, p).wait_send()

        @pl.when(y != 3)
        def _():
            halo(i, 0).wait_send()
            halo(i, 1).wait_send()

        @pl.when(y != 0)
        def _():
            land(i).wait_send()

    halo_begin(0)
    halo_half(0, 0)
    halo_half(0, 1)

    rate_col[...] = jnp.transpose(jnp.broadcast_to(rates[...], (TILE, TOK)))

    @pl.loop(0, TOK // 256)
    def _(i):
        rows = pl.ds(pl.multiple_of(i * 256, 256), 256)
        gradient_rows(rows, k, v, rate_col, wg, wl, wd, hid, scaled, g_gate, g_lift)

    def block(c, low=0, size=ROWS):
        return pl.ds(pl.multiple_of(((c + 2 * NZ) % NZ) * ROWS + low, 16), size)

    def rs_begin(s):
        go(part.at[s, block(z + 4, 0, TOP)], rbuf.at[s, 0, 0, pl.ds(0, TOP)],
           rs_s.at[s, 0, 0], rs_r.at[s, 0, 0], up)
        go(part.at[s, block(z + 4, TOP, ROWS - TOP)], rbuf.at[s, 1, 0, pl.ds(TOP, ROWS - TOP)],
           rs_s.at[s, 1, 0], rs_r.at[s, 1, 0], down)

    def rs_arrived(s, d, step):
        if step == 1:
            where = rbuf.at[s, d, 0, pl.ds(0, TOP) if d == 0 else pl.ds(TOP, ROWS - TOP)]
        else:
            where = rbuf.at[s, d, step - 1]
        remote(where, where, rs_s.at[s, d, step - 1], rs_r.at[s, d, step - 1],
               up if d == 0 else down).wait_recv()

    def rs_step(s, step):
        for d in (0, 1):
            rs_arrived(s, d, step)
            c = z + 4 - step if d == 0 else z - 4 + step
            spot = rbuf.at[s, d, step - 1]
            if step == 1:
                lo, size = (0, TOP) if d == 0 else (TOP, ROWS - TOP)
                olo, osize = (TOP, ROWS - TOP) if d == 0 else (0, TOP)
                spot[pl.ds(lo, size), :] = (
                    spot[pl.ds(lo, size), :].astype(F32) + part[s, block(c, lo, size), :].astype(F32)
                ).astype(BF16)
                spot[pl.ds(olo, osize), :] = part[s, block(c, olo, osize), :]
            else:
                spot[...] = (spot[...].astype(F32) + part[s, block(c), :].astype(F32)).astype(BF16)
            go(spot, rbuf.at[s, d, step], rs_s.at[s, d, step], rs_r.at[s, d, step],
               up if d == 0 else down)

    def rs_end(s):
        rs_arrived(s, 0, 4)
        rs_arrived(s, 1, 4)
        ybuf[s, y] = (
            part[s, block(z), :].astype(F32) + rbuf[s, 0, 3].astype(F32) + rbuf[s, 1, 3].astype(F32)
        ).astype(BF16)
        for d in range(3):
            go(ybuf.at[s, y], ybuf.at[s, y], y_s.at[s, d], y_r.at[s, d], peers[d])

    def ag_begin(s):
        for d in range(3):
            spot = ybuf.at[s, (y + 3 - d) % NY]
            remote(spot, spot, y_s.at[s, d], y_r.at[s, d], peers[d]).wait_recv()
        total = ybuf[s, 0].astype(F32) + ybuf[s, 1].astype(F32)
        total += ybuf[s, 2].astype(F32) + ybuf[s, 3].astype(F32)
        full[s, block(z), :] = total.astype(BF16)
        spot = full.at[s, block(z)]
        go(spot, spot, ag_s.at[s, 0, 0], ag_r.at[s, 0, 0], up)
        go(spot, spot, ag_s.at[s, 1, 0], ag_r.at[s, 1, 0], down)

    def ag_step(s, step):
        for d in (0, 1):
            c = z - step if d == 0 else z + step
            part_rows = (0, TOP) if d == 0 else (TOP, ROWS - TOP)
            lo, size = part_rows if step == 4 else (0, ROWS)
            spot = full.at[s, block(c, lo, size)]
            remote(spot, spot, ag_s.at[s, d, step - 1], ag_r.at[s, d, step - 1],
                   up if d == 0 else down).wait_recv()
            if step < 4:
                lo, size = part_rows if step == 3 else (0, ROWS)
                spot = full.at[s, block(c, lo, size)]
                go(spot, spot, ag_s.at[s, d, step], ag_r.at[s, d, step], up if d == 0 else down)

    def rows_of(t, low=0, size=TILE):
        return pl.ds(t * TILE + low, size)

    def own_keys():
        row = lax.broadcasted_iota(jnp.int32, (TILE, TILE), 0)
        return lax.broadcasted_iota(jnp.int32, (TILE, TILE), 1) <= row

    def head_columns(h):
        return pl.ds(pl.multiple_of(h * ATT_HD, ATT_HD), ATT_HD)

    def weights_of(t):
        rows, low, high = rows_of(t), t * TILE, (t + 1) * TILE

        @pl.loop(0, HD // ATT_HD)
        def _(h):
            cols = head_columns(h)
            first = jnp.where(ctx == 0, -1e30, 0.0).astype(F32)
            own = dot(q[rows, cols], k[pl.ds(0, high), cols], 1, 1)
            old = dot(q[rows, cols], kh[pl.ds(low, TOK - low), cols], 1, 1) + first
            blocks = [own[:, :low]] if t else []
            blocks.append(jnp.where(own_keys(), own[:, low:], old[:, :TILE]))
            if high < TOK:
                blocks.append(old[:, TILE:])
            scores = jnp.concatenate(blocks, axis=1)
            peak = jnp.max(scores, axis=1, keepdims=True)
            w = jnp.exp2((scores - peak) * EXP_SCALE)
            total = jnp.sum(w, axis=1, keepdims=True)
            pbuf[h, rows, :] = (w * (1.0 / total)).astype(BF16)

    def attend(t):
        rows, low, high = rows_of(t), t * TILE, (t + 1) * TILE

        @pl.loop(0, HD // ATT_HD)
        def _(h):
            cols = head_columns(h)
            diagonal = pbuf[h, rows, pl.ds(low, TILE)]
            zero = jnp.zeros_like(diagonal)
            value = dot(jnp.where(own_keys(), diagonal, zero), v[pl.ds(low, TILE), cols])
            value += dot(jnp.where(own_keys(), zero, diagonal), vh[pl.ds(low, TILE), cols])
            if t:
                value += dot(pbuf[h, rows, pl.ds(0, low)], v[pl.ds(0, low), cols])
            if high < TOK:
                value += dot(pbuf[h, rows, pl.ds(high, TOK - high)], vh[pl.ds(high, TOK - high), cols])
            att[rows, cols] = value

    def normalize(s):
        g = full[s].astype(F32)
        size = jnp.sqrt(jnp.sum(jnp.sum(g * g, axis=1, keepdims=True), axis=0, keepdims=True))
        x_it[...] = (g * (1.0 / (size + 1e-06))).astype(BF16)

    def iterate():
        gram[...] = dot(x_it[...], x_it[...], 1, 1).astype(BF16)
        prod[...] = dot(gram[...], x_it[...]).astype(BF16)
        second = dot(gram[...], prod[...])
        x_it[...] = (
            quintic_first * x_it[...].astype(F32)
            + quintic_second * prod[...].astype(F32)
            + quintic_third * second
        ).astype(BF16)

    def renew(s):
        initial = (wd, wl, wg)[s][...].astype(F32)
        updated = initial + x_it[...].astype(F32)
        target = jnp.sqrt(jnp.sum(initial * initial, axis=0, keepdims=True))
        current = jnp.sqrt(jnp.sum(updated * updated, axis=0, keepdims=True) + 1e-06)
        ren[s] = (updated * (target / current)).astype(BF16)

    def gradient(s):
        left, right = ((hid, scaled), (k, g_lift), (k, g_gate))[s]
        part[s] = dot(left[...], right[...], 0, 0).astype(BF16)

    gradient(0)
    rs_begin(0)
    gradient(1)
    rs_begin(1)
    gradient(2)
    rs_step(0, 1)
    rs_step(1, 1)
    rs_begin(2)
    halo_climb(0)
    rs_step(0, 2)
    rs_step(1, 2)
    rs_step(2, 1)
    halo_land(0)
    rs_step(0, 3)
    rs_step(1, 3)
    rs_step(2, 2)
    rs_end(0)
    rs_end(1)
    halo_wait(0)
    weights_of(0)
    rs_step(2, 3)
    ag_begin(0)
    weights_of(1)
    ag_begin(1)
    rs_end(2)
    halo_begin(1)
    halo_half(1, 0)
    halo_half(1, 1)
    weights_of(2)
    ag_step(0, 1)
    ag_step(1, 1)
    weights_of(3)
    ag_begin(2)
    halo_climb(1)
    ag_step(0, 2)
    ag_step(1, 2)
    ag_step(2, 1)
    halo_land(1)
    ag_step(0, 3)
    ag_step(1, 3)
    ag_step(2, 2)
    ag_step(0, 4)
    normalize(0)
    iterate()
    ag_step(2, 3)
    iterate()
    ag_step(1, 4)
    iterate()
    renew(0)
    for s in (1, 2):
        if s == 2:
            ag_step(2, 4)
        normalize(s)
        pl.loop(0, NS_ITERS)(lambda i: iterate())
        renew(s)
    halo_wait(1)

    chunks = TOK // TILE
    half = TILE // 2
    for t in range(chunks):
        attend(t)
        rows = rows_of(t)
        gate = dot(q[rows, :], ren[2])
        lift = dot(q[rows, :], ren[1])
        applied = (gate * logistic(gate) * lift).astype(BF16)
        result = dot(applied, ren[0])
        back = lax.rsqrt(jnp.mean(result * result, axis=1, keepdims=True) + 1e-06)
        cbuf[head, rows, :] = (att[rows, :] + result * back * gain[...][None, :]).astype(BF16)
        spot = cbuf.at[head, rows]
        go(spot, spot, d1_s.at[0, t], d1_r.at[0, t], right)
        go(spot, spot, d1_s.at[1, t], d1_r.at[1, t], left)
        go(spot, spot, pr_s.at[0, t], pr_r.at[0, t], partner)

    def add(i, rows, first=False, last=False):
        h = order[i]
        value = dot(cbuf[h, rows, :], wbuf[h])
        if not first:
            value += acc[rows, :]
        if last:
            out[rows, :] = value.astype(BF16)
        else:
            acc[rows, :] = value

    whole = pl.ds(0, TOK)

    def near(t):
        for d in (0, 1):
            h = place(-1) if d == 0 else place(1)
            spot = cbuf.at[h, rows_of(t)]
            arrived(spot, d1_s.at[d, t], d1_r.at[d, t], left if d == 0 else right)
            piece = cbuf.at[h, rows_of(t, d * half, half)]
            go(piece, piece, d2_s.at[d, t], d2_r.at[d, t], right if d == 0 else left)
            go(spot, spot, pr_s.at[1 + d, t], pr_r.at[1 + d, t], partner)

    def far(t):
        h = place(2)
        for d in (0, 1):
            piece = cbuf.at[h, rows_of(t, d * half, half)]
            arrived(piece, d2_s.at[d, t], d2_r.at[d, t], left if d == 0 else right)
        spot = cbuf.at[h, rows_of(t)]
        go(spot, spot, pr_s.at[3, t], pr_r.at[3, t], partner)

    def mirrored(j, t):
        h = place((0, -1, 1, 2)[j], 1)
        spot = cbuf.at[h, rows_of(t)]
        arrived(spot, pr_s.at[j, t], pr_r.at[j, t], partner)

    near(0)
    loads[0].wait()
    add(0, whole, first=True)
    near(1)
    for t in range(chunks):
        mirrored(0, t)
    loads[1].wait()
    add(1, whole)
    near(2)
    near(3)
    far(0)
    loads[2].wait()
    add(2, whole)
    far(1)
    loads[3].wait()
    add(3, whole)
    for t in range(chunks):
        mirrored(1, t)
    loads[4].wait()
    add(4, whole)
    far(2)
    for t in range(chunks):
        mirrored(2, t)
    loads[5].wait()
    add(5, whole)
    loads[6].wait()
    add(6, pl.ds(0, 3 * TILE))
    for t in range(chunks - 1):
        mirrored(3, t)
    loads[7].wait()
    add(7, pl.ds(0, 3 * TILE), last=True)
    far(3)
    add(6, rows_of(3))
    mirrored(3, 3)
    add(7, rows_of(3), last=True)
    for copy in started:
        copy.wait_send()
    halo_sent(0)
    halo_sent(1)


def layer(queries, key_rows, value_rows, rates, fast_gate, fast_lift, fast_down, gain, weight):
    vmem = pl.BlockSpec(memory_space=pltpu.VMEM)
    dma = pltpu.SemaphoreType.DMA
    square = (HD, HD)
    tokens = (TOK, HD)
    heads = 2 * NX
    chunks = TOK // TILE
    return pl.pallas_call(
        layer_kernel,
        name="layer",
        out_shape=jax.ShapeDtypeStruct(tokens, BF16),
        in_specs=[vmem] * 8 + [pl.BlockSpec(memory_space=pl.ANY)],
        out_specs=vmem,
        scratch_shapes=[
            pltpu.VMEM((3, HD, HD), BF16),
            pltpu.VMEM((3, 2, 4, ROWS, HD), BF16),
            pltpu.VMEM((3, NY, ROWS, HD), BF16),
            pltpu.VMEM((3, HD, HD), BF16),
            pltpu.VMEM(tokens, BF16),
            pltpu.VMEM(tokens, BF16),
            pltpu.VMEM((2, 2, TILE, HD), BF16),
            pltpu.VMEM((HD // ATT_HD, TOK, TOK), BF16),
            pltpu.VMEM(tokens, BF16),
            pltpu.VMEM(tokens, BF16),
            pltpu.VMEM(tokens, BF16),
            pltpu.VMEM(tokens, BF16),
            pltpu.VMEM(square, BF16),
            pltpu.VMEM(square, BF16),
            pltpu.VMEM(square, BF16),
            pltpu.VMEM((TOK, TILE), F32),
            pltpu.VMEM(tokens, F32),
            pltpu.VMEM((3, HD, HD), BF16),
            pltpu.VMEM((heads, TOK, HD), BF16),
            pltpu.VMEM((heads, HD, HD), BF16),
            pltpu.VMEM(tokens, F32),
            dma((2, 2)), dma((2,)),
            dma((2, 5)), dma((2, 2)),
            dma((3, 2, 4)), dma((3, 2, 4)),
            dma((3, 3)), dma((3, 3)),
            dma((3, 2, 4)), dma((3, 2, 4)),
            dma((heads,)),
            dma((2, chunks)), dma((2, chunks)),
            dma((2, chunks)), dma((2, chunks)),
            dma((4, chunks)), dma((4, chunks)),
        ],
        compiler_params=pltpu.CompilerParams(
            collective_id=0, has_side_effects=True, vmem_limit_bytes=60 * 1024 * 1024
        ),
    )(queries, key_rows, value_rows, rates, fast_gate, fast_lift, fast_down, gain, weight)


def on_device(
    queries, key_rows, value_rows, learning_rates, fast_gate, fast_lift, fast_down, output_gain, output_weight
):
    return layer(
        queries, key_rows, value_rows, learning_rates, fast_gate[0], fast_lift[0], fast_down[0],
        output_gain, output_weight.reshape(2 * NX, HD, HD),
    )


def solution(mesh):
    return jax.shard_map(
        on_device,
        mesh=mesh,
        in_specs=(
            P("ctx", "head"),
            P("ctx", "head"),
            P("ctx", "head"),
            P("head", "ctx"),
            P("head", None, None),
            P("head", None, None),
            P("head", None, None),
            P("head"),
            P(None, "head"),
        ),
        out_specs=P("ctx", "head"),
        check_vma=False,
    )
```

```python
import math

import jax
import jax.numpy as jnp
from jax import lax
from jax.experimental import pallas as pl
from jax.experimental.pallas import tpu as pltpu
from jax.sharding import PartitionSpec as P

HD = 640
ATT_HD = 128
NS_ITERS = 3
TOK = 512
NZ, NY, NX = 8, 4, 4
ROWS = HD // NZ
TOP = 48
TILE = 128
MESH = pl.DeviceIdType.MESH
BF16 = jnp.bfloat16
F32 = jnp.float32

EXP_SCALE = ATT_HD ** (-0.5) * math.log2(math.e)

quintic_first = 3.4445
quintic_second = -4.775
quintic_third = 2.0315


def dot(a, b, ca=1, cb=0):
    return lax.dot_general(a, b, (((ca,), (cb,)), ((), ())), preferred_element_type=F32)


def logistic(x):
    return 1.0 / (1.0 + jnp.exp(-x))


def remote(src, dst, send_sem, recv_sem, device):
    return pltpu.make_async_remote_copy(
        src_ref=src, dst_ref=dst, send_sem=send_sem, recv_sem=recv_sem,
        device_id=device, device_id_type=MESH,
    )


def gradient_rows(rows, k, v, rates, wg, wl, wd, hid, scaled, g_gate, g_lift):
    keys = k[rows, :]
    gate_pre = dot(keys, wg[...])
    lift_pre = dot(keys, wl[...])
    sig = logistic(gate_pre)
    silu = gate_pre * sig
    hid[rows, :] = (silu * lift_pre).astype(BF16)
    sc = (rates[rows, :1] * v[rows, :].astype(F32)).astype(BF16)
    scaled[rows, :] = sc
    backward = dot(sc, wd[...], 1, 1)
    g_gate[rows, :] = (backward * lift_pre * (sig * (1.0 + gate_pre * (1.0 - sig)))).astype(BF16)
    g_lift[rows, :] = (backward * silu).astype(BF16)


def layer_kernel(
    q, k, v, rates, wg, wl, wd, gain, weight,
    out,
    part, rbuf, ybuf, full, kh, vh, relay, pbuf, hid, scaled, g_gate, g_lift, gram, prod, x_it,
    rate_col, att, ren, cbuf, wown, wbuf, acc, acc_other, o_out, o_in,
    halo_s, halo_r, x_s, x_r, rs_s, rs_r, y_s, y_r, ag_s, ag_r,
    w_sem, wx_s, wx_r, d1_s, d1_r, d2_s, d2_r, pr_s, pr_r, o_s, o_r,
):
    ctx = lax.axis_index("ctx")
    z, y = ctx // NY, ctx % NY
    up = {"ctx": ((z + 1) % NZ) * NY + y}
    down = {"ctx": ((z + NZ - 1) % NZ) * NY + y}
    peers = [{"ctx": z * NY + (y + d) % NY} for d in (1, 2, 3)]
    after = {"ctx": z * NY + (y + 1) % NY}
    head = lax.axis_index("head")
    x, core = head // 2, head % 2

    def place(offset, other=0):
        side = (core + other) % 2
        return ((x + offset + NX) % NX) * 2 + side

    right, left, partner = ({"head": place(1)}, {"head": place(-1)}, {"head": place(0, 1)})
    started = []

    def go(*args):
        copy = remote(*args)
        copy.start()
        started.append(copy)
        return copy

    def arrived(spot, send_sem, recv_sem, device):
        remote(spot, spot, send_sem, recv_sem, device).wait_recv()

    def chip(offset):
        return (x + offset + NX) % NX

    order = [head, place(0, 1)] + [chip(offset) * 2 + p for offset in (-1, 1, 2) for p in (0, 1)]
    loads = [pltpu.make_async_copy(weight.at[h], wown.at[h], w_sem.at[i]) for i, h in enumerate(order)]

    barrier = pltpu.get_barrier_semaphore()
    sides = [{"head": chip(offset) * 2 + p} for offset in (-1, 1) for p in (0, 1)]
    everyone = [up, down, partner] + peers + sides
    for device in everyone:
        pl.semaphore_signal(barrier, inc=1, device_id=device, device_id_type=MESH)
    pl.semaphore_wait(barrier, len(everyone))

    def piece(p):
        return pl.ds(p * TILE, TILE)

    def mine():
        return pl.ds(pl.multiple_of(y * TILE, TILE), TILE)

    def halo(i, half):
        source, target = ((k, kh), (v, vh))[i]
        rows = pl.ds(half * (TOK // 2), TOK // 2)
        return remote(source.at[rows], target.at[rows], halo_s.at[i, half], halo_r.at[i], after)

    def across(i, p):
        source = (k, v)[i]
        return remote(source.at[piece(p)], relay.at[i, 0], x_s.at[i, p], x_r.at[i, 0], {"ctx": z * NY + p})

    def climb(i, column):
        source, target = ((k, kh), (v, vh))[i]
        if column == 3:
            return remote(source.at[piece(3)], relay.at[i, 1], x_s.at[i, 3], x_r.at[i, 1], up)
        if column == 0:
            return remote(relay.at[i, 0], target.at[piece(0)], x_s.at[i, 3], halo_r.at[i], up)
        return remote(relay.at[i, 0], relay.at[i, 1], x_s.at[i, 3], x_r.at[i, 1], up)

    def land(i):
        target = (kh, vh)[i]
        return remote(relay.at[i, 1], target.at[mine()], x_s.at[i, 4], halo_r.at[i], {"ctx": z * NY})

    def halo_begin(i):
        @pl.when(y == 3)
        def _():
            for p in range(3):
                across(i, p).start()
            climb(i, 3).start()

    def halo_half(i, half):
        @pl.when(y != 3)
        def _():
            halo(i, half).start()

    def halo_climb(i):
        @pl.when(y != 3)
        def _():
            across(i, 0).wait_recv()

        @pl.when(y == 0)
        def _():
            climb(i, 0).start()

        @pl.when((y == 1) | (y == 2))
        def _():
            climb(i, 1).start()

    def halo_land(i):
        @pl.when(y != 0)
        def _():
            climb(i, 1).wait_recv()
            land(i).start()

    def halo_wait(i):
        target = (kh, vh)[i]
        remote(target, target, halo_s.at[i, 0], halo_r.at[i], after).wait_recv()

    def halo_sent(i):
        climb(i, 1).wait_send()

        @pl.when(y == 3)
        def _():
            for p in range(3):
                across(i, p).wait_send()

        @pl.when(y != 3)
        def _():
            halo(i, 0).wait_send()
            halo(i, 1).wait_send()

        @pl.when(y != 0)
        def _():
            land(i).wait_send()

    halo_begin(0)
    halo_half(0, 0)
    halo_half(0, 1)

    for h in range(2 * NX):
        go(weight.at[h], wbuf.at[h], wx_s.at[h], wx_r.at[h], partner)
    for load in loads:
        load.start()
    rate_col[...] = jnp.transpose(jnp.broadcast_to(rates[...], (TILE, TOK)))

    @pl.loop(0, TOK // 256)
    def _(i):
        rows = pl.ds(pl.multiple_of(i * 256, 256), 256)
        gradient_rows(rows, k, v, rate_col, wg, wl, wd, hid, scaled, g_gate, g_lift)

    def block(c, low=0, size=ROWS):
        return pl.ds(pl.multiple_of(((c + 2 * NZ) % NZ) * ROWS + low, 16), size)

    def rs_begin(s):
        go(part.at[s, block(z + 4, 0, TOP)], rbuf.at[s, 0, 0, pl.ds(0, TOP)],
           rs_s.at[s, 0, 0], rs_r.at[s, 0, 0], up)
        go(part.at[s, block(z + 4, TOP, ROWS - TOP)], rbuf.at[s, 1, 0, pl.ds(TOP, ROWS - TOP)],
           rs_s.at[s, 1, 0], rs_r.at[s, 1, 0], down)

    def rs_arrived(s, d, step):
        if step == 1:
            where = rbuf.at[s, d, 0, pl.ds(0, TOP) if d == 0 else pl.ds(TOP, ROWS - TOP)]
        else:
            where = rbuf.at[s, d, step - 1]
        remote(where, where, rs_s.at[s, d, step - 1], rs_r.at[s, d, step - 1],
               up if d == 0 else down).wait_recv()

    def rs_step(s, step):
        for d in (0, 1):
            rs_arrived(s, d, step)
            c = z + 4 - step if d == 0 else z - 4 + step
            spot = rbuf.at[s, d, step - 1]
            if step == 1:
                lo, size = (0, TOP) if d == 0 else (TOP, ROWS - TOP)
                olo, osize = (TOP, ROWS - TOP) if d == 0 else (0, TOP)
                spot[pl.ds(lo, size), :] = (
                    spot[pl.ds(lo, size), :].astype(F32) + part[s, block(c, lo, size), :].astype(F32)
                ).astype(BF16)
                spot[pl.ds(olo, osize), :] = part[s, block(c, olo, osize), :]
            else:
                spot[...] = (spot[...].astype(F32) + part[s, block(c), :].astype(F32)).astype(BF16)
            go(spot, rbuf.at[s, d, step], rs_s.at[s, d, step], rs_r.at[s, d, step],
               up if d == 0 else down)

    def rs_end(s):
        rs_arrived(s, 0, 4)
        rs_arrived(s, 1, 4)
        ybuf[s, y] = (
            part[s, block(z), :].astype(F32) + rbuf[s, 0, 3].astype(F32) + rbuf[s, 1, 3].astype(F32)
        ).astype(BF16)
        for d in range(3):
            go(ybuf.at[s, y], ybuf.at[s, y], y_s.at[s, d], y_r.at[s, d], peers[d])

    def ag_begin(s):
        for d in range(3):
            spot = ybuf.at[s, (y + 3 - d) % NY]
            remote(spot, spot, y_s.at[s, d], y_r.at[s, d], peers[d]).wait_recv()
        total = ybuf[s, 0].astype(F32) + ybuf[s, 1].astype(F32)
        total += ybuf[s, 2].astype(F32) + ybuf[s, 3].astype(F32)
        full[s, block(z), :] = total.astype(BF16)
        spot = full.at[s, block(z)]
        go(spot, spot, ag_s.at[s, 0, 0], ag_r.at[s, 0, 0], up)
        go(spot, spot, ag_s.at[s, 1, 0], ag_r.at[s, 1, 0], down)

    def ag_step(s, step):
        for d in (0, 1):
            c = z - step if d == 0 else z + step
            part_rows = (0, TOP) if d == 0 else (TOP, ROWS - TOP)
            lo, size = part_rows if step == 4 else (0, ROWS)
            spot = full.at[s, block(c, lo, size)]
            remote(spot, spot, ag_s.at[s, d, step - 1], ag_r.at[s, d, step - 1],
                   up if d == 0 else down).wait_recv()
            if step < 4:
                lo, size = part_rows if step == 3 else (0, ROWS)
                spot = full.at[s, block(c, lo, size)]
                go(spot, spot, ag_s.at[s, d, step], ag_r.at[s, d, step], up if d == 0 else down)

    def rows_of(t, low=0, size=TILE):
        return pl.ds(t * TILE + low, size)

    def own_keys():
        row = lax.broadcasted_iota(jnp.int32, (TILE, TILE), 0)
        return lax.broadcasted_iota(jnp.int32, (TILE, TILE), 1) <= row

    def head_columns(h):
        return pl.ds(pl.multiple_of(h * ATT_HD, ATT_HD), ATT_HD)

    def weights_of(t, begin=0, end=HD // ATT_HD):
        rows, low, high = rows_of(t), t * TILE, (t + 1) * TILE

        @pl.loop(begin, end)
        def _(h):
            cols = head_columns(h)
            first = jnp.where(ctx == 0, -1e30, 0.0).astype(F32)
            own = dot(q[rows, cols], k[pl.ds(0, high), cols], 1, 1)
            old = dot(q[rows, cols], kh[pl.ds(low, TOK - low), cols], 1, 1) + first
            blocks = [own[:, :low]] if t else []
            blocks.append(jnp.where(own_keys(), own[:, low:], old[:, :TILE]))
            if high < TOK:
                blocks.append(old[:, TILE:])
            scores = jnp.concatenate(blocks, axis=1)
            peak = jnp.max(scores, axis=1, keepdims=True)
            w = jnp.exp2((scores - peak) * EXP_SCALE)
            total = jnp.sum(w, axis=1, keepdims=True)
            pbuf[h, rows, :] = (w * (1.0 / total)).astype(BF16)

    def attend(t):
        rows, low, high = rows_of(t), t * TILE, (t + 1) * TILE

        @pl.loop(0, HD // ATT_HD)
        def _(h):
            cols = head_columns(h)
            diagonal = pbuf[h, rows, pl.ds(low, TILE)]
            zero = jnp.zeros_like(diagonal)
            value = dot(jnp.where(own_keys(), diagonal, zero), v[pl.ds(low, TILE), cols])
            value += dot(jnp.where(own_keys(), zero, diagonal), vh[pl.ds(low, TILE), cols])
            if t:
                value += dot(pbuf[h, rows, pl.ds(0, low)], v[pl.ds(0, low), cols])
            if high < TOK:
                value += dot(pbuf[h, rows, pl.ds(high, TOK - high)], vh[pl.ds(high, TOK - high), cols])
            att[rows, cols] = value

    def normalize(s):
        g = full[s].astype(F32)
        size = jnp.sqrt(jnp.sum(jnp.sum(g * g, axis=1, keepdims=True), axis=0, keepdims=True))
        x_it[...] = (g * (1.0 / (size + 1e-06))).astype(BF16)

    def iterate():
        gram[...] = dot(x_it[...], x_it[...], 1, 1).astype(BF16)
        prod[...] = dot(gram[...], x_it[...]).astype(BF16)
        second = dot(gram[...], prod[...])
        x_it[...] = (
            quintic_first * x_it[...].astype(F32)
            + quintic_second * prod[...].astype(F32)
            + quintic_third * second
        ).astype(BF16)

    def renew(s):
        initial = (wd, wl, wg)[s][...].astype(F32)
        updated = initial + x_it[...].astype(F32)
        target = jnp.sqrt(jnp.sum(initial * initial, axis=0, keepdims=True))
        current = jnp.sqrt(jnp.sum(updated * updated, axis=0, keepdims=True) + 1e-06)
        ren[s] = (updated * (target / current)).astype(BF16)

    def gradient(s):
        left, right = ((hid, scaled), (k, g_lift), (k, g_gate))[s]
        part[s] = dot(left[...], right[...], 0, 0).astype(BF16)

    gradient(0)
    rs_begin(0)
    gradient(1)
    gradient(2)
    rs_step(0, 1)
    rs_begin(1)
    rs_begin(2)
    rs_step(0, 2)
    rs_step(1, 1)
    rs_step(2, 1)
    halo_climb(0)
    rs_step(0, 3)
    rs_step(1, 2)
    rs_step(2, 2)
    halo_land(0)
    rs_end(0)
    rs_step(1, 3)
    rs_step(2, 3)
    rs_end(1)
    halo_wait(0)
    weights_of(0, 0, 3)
    ag_begin(0)
    weights_of(0, 3, 5)
    rs_end(2)
    halo_begin(1)
    halo_half(1, 0)
    halo_half(1, 1)
    weights_of(1, 0, 3)
    ag_step(0, 1)
    weights_of(1, 3, 5)
    ag_begin(1)
    weights_of(2, 0, 3)
    ag_step(0, 2)
    halo_climb(1)
    weights_of(2, 3, 5)
    ag_begin(2)
    weights_of(3, 0, 3)
    ag_step(1, 1)
    weights_of(3, 3, 5)
    ag_step(0, 3)
    ag_step(2, 1)
    ag_step(1, 2)
    ag_step(0, 4)
    normalize(0)
    iterate()
    ag_step(2, 2)
    iterate()
    ag_step(1, 3)
    halo_land(1)
    iterate()
    ag_step(2, 3)
    renew(0)
    ag_step(1, 4)
    normalize(1)
    iterate()
    ag_step(2, 4)
    iterate()
    iterate()
    renew(1)
    normalize(2)
    iterate()
    iterate()
    iterate()
    renew(2)
    halo_wait(1)

    chunks = TOK // TILE
    half = TILE // 2
    for t in (0, 2, 1, 3):
        attend(t)
        rows = rows_of(t)
        gate = dot(q[rows, :], ren[2])
        lift = dot(q[rows, :], ren[1])
        applied = (gate * logistic(gate) * lift).astype(BF16)
        result = dot(applied, ren[0])
        back = lax.rsqrt(jnp.mean(result * result, axis=1, keepdims=True) + 1e-06)
        cbuf[head, rows, :] = (att[rows, :] + result * back * gain[...][None, :]).astype(BF16)
        spot = cbuf.at[head, rows]
        side, c = t // 2, t % 2
        go(spot, spot, d1_s.at[0, t], d1_r.at[0, core, c], {"head": chip(1) * 2 + side})
        go(spot, spot, d1_s.at[1, t], d1_r.at[1, core, c], {"head": chip(-1) * 2 + side})

        @pl.when(core != side)
        def _():
            remote(spot, spot, pr_s.at[c], pr_r.at[c], partner).start()

    def here(c, low=0, size=TILE):
        return pl.ds(pl.multiple_of(core * 2 * TILE + c * TILE + low, half), size)

    def near(c):
        for p in (0, 1):
            for d in (0, 1):
                h = chip(2 * d - 1) * 2 + p
                spot = cbuf.at[h, here(c)]
                arrived(spot, d1_s.at[d, 0], d1_r.at[d, p, c], left if d == 0 else right)
                piece = cbuf.at[h, here(c, d * half, half)]
                go(piece, piece, d2_s.at[d, p, c], d2_r.at[d, p, c], right if d == 0 else left)

    def far(p, c):
        for d in (0, 1):
            piece = cbuf.at[chip(2) * 2 + p, here(c, d * half, half)]
            arrived(piece, d2_s.at[d, p, c], d2_r.at[d, p, c], left if d == 0 else right)

    def mirrored(c):
        spot = cbuf.at[place(0, 1), here(c)]
        arrived(spot, pr_s.at[c], pr_r.at[c], partner)

    def add(i, c=None, first=False, last=False):
        h = order[i]
        rows = pl.ds(core * 2 * TILE, 2 * TILE) if c is None else here(c)
        spot = pl.ds(0, 2 * TILE) if c is None else pl.ds(c * TILE, TILE)
        tokens = cbuf[h, rows, :]
        for matrix, total, result in ((wbuf, acc_other, o_out), (wown, acc, None)):
            value = dot(tokens, matrix[h])
            if not first:
                value += total[spot, :]
            if not last:
                total[spot, :] = value
            elif result is None:
                out[rows, :] = value.astype(BF16)
            else:
                result[spot, :] = value.astype(BF16)
                go(o_out.at[spot], o_in.at[spot], o_s.at[c], o_r.at[c], partner)

    def weights_here(i):
        h = order[i]
        loads[i].wait()
        arrived(wbuf.at[h], wx_s.at[h], wx_r.at[h], partner)

    for i in range(2 * NX):
        weights_here(i)
    near(0)
    add(0, first=True)
    for c in (0, 1):
        mirrored(c)
    add(1)
    near(1)
    for i in (2, 3, 4, 5):
        add(i)
    for c in (0, 1):
        for p in (0, 1):
            far(p, c)
            add(6 + p, c, last=p == 1)
    other = pl.ds(pl.multiple_of((1 - core) * 2 * TILE, 2 * TILE), 2 * TILE)
    for c in (0, 1):
        spot = o_in.at[pl.ds(c * TILE, TILE)]
        arrived(spot, o_s.at[c], o_r.at[c], partner)
    out[other, :] = o_in[...]
    for copy in started:
        copy.wait_send()
    for c in (0, 1):
        spot = cbuf.at[head, rows_of(c)]
        remote(spot, spot, pr_s.at[c], pr_r.at[c], partner).wait_send()
    halo_sent(0)
    halo_sent(1)


def layer(queries, key_rows, value_rows, rates, fast_gate, fast_lift, fast_down, gain, weight):
    vmem = pl.BlockSpec(memory_space=pltpu.VMEM)
    dma = pltpu.SemaphoreType.DMA
    square = (HD, HD)
    tokens = (TOK, HD)
    heads = 2 * NX
    chunks = TOK // TILE
    return pl.pallas_call(
        layer_kernel,
        name="layer",
        out_shape=jax.ShapeDtypeStruct(tokens, BF16),
        in_specs=[vmem] * 8 + [pl.BlockSpec(memory_space=pl.ANY)],
        out_specs=vmem,
        scratch_shapes=[
            pltpu.VMEM((3, HD, HD), BF16),
            pltpu.VMEM((3, 2, 4, ROWS, HD), BF16),
            pltpu.VMEM((3, NY, ROWS, HD), BF16),
            pltpu.VMEM((3, HD, HD), BF16),
            pltpu.VMEM(tokens, BF16),
            pltpu.VMEM(tokens, BF16),
            pltpu.VMEM((2, 2, TILE, HD), BF16),
            pltpu.VMEM((HD // ATT_HD, TOK, TOK), BF16),
            pltpu.VMEM(tokens, BF16),
            pltpu.VMEM(tokens, BF16),
            pltpu.VMEM(tokens, BF16),
            pltpu.VMEM(tokens, BF16),
            pltpu.VMEM(square, BF16),
            pltpu.VMEM(square, BF16),
            pltpu.VMEM(square, BF16),
            pltpu.VMEM((TOK, TILE), F32),
            pltpu.VMEM(tokens, F32),
            pltpu.VMEM((3, HD, HD), BF16),
            pltpu.VMEM((heads, TOK, HD), BF16),
            pltpu.VMEM((heads, HD, HD), BF16),
            pltpu.VMEM((heads, HD, HD), BF16),
            pltpu.VMEM((TOK // 2, HD), F32),
            pltpu.VMEM((TOK // 2, HD), F32),
            pltpu.VMEM((TOK // 2, HD), BF16),
            pltpu.VMEM((TOK // 2, HD), BF16),
            dma((2, 2)), dma((2,)),
            dma((2, 5)), dma((2, 2)),
            dma((3, 2, 4)), dma((3, 2, 4)),
            dma((3, 3)), dma((3, 3)),
            dma((3, 2, 4)), dma((3, 2, 4)),
            dma((heads,)),
            dma((heads,)), dma((heads,)),
            dma((2, chunks)), dma((2, 2, 2)),
            dma((2, 2, 2)), dma((2, 2, 2)),
            dma((2,)), dma((2,)),
            dma((2,)), dma((2,)),
        ],
        compiler_params=pltpu.CompilerParams(
            collective_id=0, has_side_effects=True, vmem_limit_bytes=60 * 1024 * 1024
        ),
    )(queries, key_rows, value_rows, rates, fast_gate, fast_lift, fast_down, gain, weight)


def on_device(
    queries, key_rows, value_rows, learning_rates, fast_gate, fast_lift, fast_down, output_gain, output_weight
):
    return layer(
        queries, key_rows, value_rows, learning_rates, fast_gate[0], fast_lift[0], fast_down[0],
        output_gain, output_weight.reshape(2 * NX, HD, HD),
    )


def solution(mesh):
    return jax.shard_map(
        on_device,
        mesh=mesh,
        in_specs=(
            P("ctx", "head"),
            P("ctx", "head"),
            P("ctx", "head"),
            P("head", "ctx"),
            P("head", None, None),
            P("head", None, None),
            P("head", None, None),
            P("head"),
            P(None, "head"),
        ),
        out_specs=P("ctx", "head"),
        check_vma=False,
    )
```

```python
import math

import jax
import jax.numpy as jnp
from jax import lax
from jax.experimental import pallas as pl
from jax.experimental.pallas import tpu as pltpu
from jax.sharding import PartitionSpec as P

HD = 640
ATT_HD = 128
NS_ITERS = 3
TOK = 512
NZ, NY, NX = 8, 4, 4
ROWS = HD // NZ
TOP = 48
TILE = 128
MESH = pl.DeviceIdType.MESH
BF16 = jnp.bfloat16
F32 = jnp.float32

EXP_SCALE = ATT_HD ** (-0.5) * math.log2(math.e)

quintic_first = 3.4445
quintic_second = -4.775
quintic_third = 2.0315


def dot(a, b, ca=1, cb=0):
    return lax.dot_general(a, b, (((ca,), (cb,)), ((), ())), preferred_element_type=F32)


def logistic(x):
    return 1.0 / (1.0 + jnp.exp(-x))


def remote(src, dst, send_sem, recv_sem, device):
    return pltpu.make_async_remote_copy(
        src_ref=src, dst_ref=dst, send_sem=send_sem, recv_sem=recv_sem,
        device_id=device, device_id_type=MESH,
    )


def gradient_rows(rows, k, v, rates, wg, wl, wd, hid, scaled, g_gate, g_lift):
    keys = k[rows, :]
    gate_pre = dot(keys, wg[...])
    lift_pre = dot(keys, wl[...])
    sig = logistic(gate_pre)
    silu = gate_pre * sig
    hid[rows, :] = (silu * lift_pre).astype(BF16)
    sc = (rates[rows, :1] * v[rows, :].astype(F32)).astype(BF16)
    scaled[rows, :] = sc
    backward = dot(sc, wd[...], 1, 1)
    g_gate[rows, :] = (backward * lift_pre * (sig * (1.0 + gate_pre * (1.0 - sig)))).astype(BF16)
    g_lift[rows, :] = (backward * silu).astype(BF16)


def layer_kernel(
    q, k, v, rates, wg, wl, wd, gain, weight,
    out,
    part, rbuf, ybuf, full, kh, vh, relay, pbuf, hid, scaled, g_gate, g_lift, gram, prod, x_it,
    rate_col, att, ren, cbuf, wown, wbuf, acc, acc_other, o_out, o_in,
    halo_s, halo_r, x_s, x_r, rs_s, rs_r, y_s, y_r, ag_s, ag_r,
    w_sem, wx_s, wx_r, d1_s, d1_r, d2_s, d2_r, pr_s, pr_r, o_s, o_r,
):
    ctx = lax.axis_index("ctx")
    z, y = ctx // NY, ctx % NY
    up = {"ctx": ((z + 1) % NZ) * NY + y}
    down = {"ctx": ((z + NZ - 1) % NZ) * NY + y}
    peers = [{"ctx": z * NY + (y + d) % NY} for d in (1, 2, 3)]
    after = {"ctx": z * NY + (y + 1) % NY}
    head = lax.axis_index("head")
    x, core = head // 2, head % 2

    def place(offset, other=0):
        side = (core + other) % 2
        return ((x + offset + NX) % NX) * 2 + side

    right, left, partner = ({"head": place(1)}, {"head": place(-1)}, {"head": place(0, 1)})
    started = []

    def go(*args):
        copy = remote(*args)
        copy.start()
        started.append(copy)
        return copy

    def arrived(spot, send_sem, recv_sem, device):
        remote(spot, spot, send_sem, recv_sem, device).wait_recv()

    def chip(offset):
        return (x + offset + NX) % NX

    order = [head, place(0, 1)] + [chip(offset) * 2 + p for offset in (-1, 1, 2) for p in (0, 1)]
    loads = [pltpu.make_async_copy(weight.at[h], wown.at[h], w_sem.at[i]) for i, h in enumerate(order)]

    barrier = pltpu.get_barrier_semaphore()
    sides = [{"head": chip(offset) * 2 + p} for offset in (-1, 1) for p in (0, 1)]
    everyone = [up, down, partner] + peers + sides
    for device in everyone:
        pl.semaphore_signal(barrier, inc=1, device_id=device, device_id_type=MESH)
    pl.semaphore_wait(barrier, len(everyone))

    def piece(p):
        return pl.ds(p * TILE, TILE)

    def mine():
        return pl.ds(pl.multiple_of(y * TILE, TILE), TILE)

    def halo(i, half):
        source, target = ((k, kh), (v, vh))[i]
        rows = pl.ds(half * (TOK // 2), TOK // 2)
        return remote(source.at[rows], target.at[rows], halo_s.at[i, half], halo_r.at[i], after)

    def across(i, p):
        source = (k, v)[i]
        return remote(source.at[piece(p)], relay.at[i, 0], x_s.at[i, p], x_r.at[i, 0], {"ctx": z * NY + p})

    def climb(i, column):
        source, target = ((k, kh), (v, vh))[i]
        if column == 3:
            return remote(source.at[piece(3)], relay.at[i, 1], x_s.at[i, 3], x_r.at[i, 1], up)
        if column == 0:
            return remote(relay.at[i, 0], target.at[piece(0)], x_s.at[i, 3], halo_r.at[i], up)
        return remote(relay.at[i, 0], relay.at[i, 1], x_s.at[i, 3], x_r.at[i, 1], up)

    def land(i):
        target = (kh, vh)[i]
        return remote(relay.at[i, 1], target.at[mine()], x_s.at[i, 4], halo_r.at[i], {"ctx": z * NY})

    def halo_begin(i):
        @pl.when(y == 3)
        def _():
            for p in range(3):
                across(i, p).start()
            climb(i, 3).start()

    def halo_half(i, half):
        @pl.when(y != 3)
        def _():
            halo(i, half).start()

    def halo_climb(i):
        @pl.when(y != 3)
        def _():
            across(i, 0).wait_recv()

        @pl.when(y == 0)
        def _():
            climb(i, 0).start()

        @pl.when((y == 1) | (y == 2))
        def _():
            climb(i, 1).start()

    def halo_land(i):
        @pl.when(y != 0)
        def _():
            climb(i, 1).wait_recv()
            land(i).start()

    def halo_wait(i):
        target = (kh, vh)[i]
        remote(target, target, halo_s.at[i, 0], halo_r.at[i], after).wait_recv()

    def halo_sent(i):
        climb(i, 1).wait_send()

        @pl.when(y == 3)
        def _():
            for p in range(3):
                across(i, p).wait_send()

        @pl.when(y != 3)
        def _():
            halo(i, 0).wait_send()
            halo(i, 1).wait_send()

        @pl.when(y != 0)
        def _():
            land(i).wait_send()

    halo_begin(0)
    halo_half(0, 0)
    halo_half(0, 1)

    rate_col[...] = jnp.transpose(jnp.broadcast_to(rates[...], (TILE, TOK)))

    @pl.loop(0, TOK // 256)
    def _(i):
        rows = pl.ds(pl.multiple_of(i * 256, 256), 256)
        gradient_rows(rows, k, v, rate_col, wg, wl, wd, hid, scaled, g_gate, g_lift)

    def block(c, low=0, size=ROWS):
        return pl.ds(pl.multiple_of(((c + 2 * NZ) % NZ) * ROWS + low, 16), size)

    def rs_begin(s):
        go(part.at[s, block(z + 4, 0, TOP)], rbuf.at[s, 0, 0, pl.ds(0, TOP)],
           rs_s.at[s, 0, 0], rs_r.at[s, 0, 0], up)
        go(part.at[s, block(z + 4, TOP, ROWS - TOP)], rbuf.at[s, 1, 0, pl.ds(TOP, ROWS - TOP)],
           rs_s.at[s, 1, 0], rs_r.at[s, 1, 0], down)

    def rs_arrived(s, d, step):
        if step == 1:
            where = rbuf.at[s, d, 0, pl.ds(0, TOP) if d == 0 else pl.ds(TOP, ROWS - TOP)]
        else:
            where = rbuf.at[s, d, step - 1]
        remote(where, where, rs_s.at[s, d, step - 1], rs_r.at[s, d, step - 1],
               up if d == 0 else down).wait_recv()

    def rs_step(s, step):
        for d in (0, 1):
            rs_arrived(s, d, step)
            c = z + 4 - step if d == 0 else z - 4 + step
            spot = rbuf.at[s, d, step - 1]
            if step == 1:
                lo, size = (0, TOP) if d == 0 else (TOP, ROWS - TOP)
                olo, osize = (TOP, ROWS - TOP) if d == 0 else (0, TOP)
                spot[pl.ds(lo, size), :] = (
                    spot[pl.ds(lo, size), :].astype(F32) + part[s, block(c, lo, size), :].astype(F32)
                ).astype(BF16)
                spot[pl.ds(olo, osize), :] = part[s, block(c, olo, osize), :]
            else:
                spot[...] = (spot[...].astype(F32) + part[s, block(c), :].astype(F32)).astype(BF16)
            go(spot, rbuf.at[s, d, step], rs_s.at[s, d, step], rs_r.at[s, d, step],
               up if d == 0 else down)

    def rs_end(s):
        rs_arrived(s, 0, 4)
        rs_arrived(s, 1, 4)
        ybuf[s, y] = (
            part[s, block(z), :].astype(F32) + rbuf[s, 0, 3].astype(F32) + rbuf[s, 1, 3].astype(F32)
        ).astype(BF16)
        for d in range(3):
            go(ybuf.at[s, y], ybuf.at[s, y], y_s.at[s, d], y_r.at[s, d], peers[d])

    def ag_begin(s):
        for d in range(3):
            spot = ybuf.at[s, (y + 3 - d) % NY]
            remote(spot, spot, y_s.at[s, d], y_r.at[s, d], peers[d]).wait_recv()
        total = ybuf[s, 0].astype(F32) + ybuf[s, 1].astype(F32)
        total += ybuf[s, 2].astype(F32) + ybuf[s, 3].astype(F32)
        full[s, block(z), :] = total.astype(BF16)
        spot = full.at[s, block(z)]
        go(spot, spot, ag_s.at[s, 0, 0], ag_r.at[s, 0, 0], up)
        go(spot, spot, ag_s.at[s, 1, 0], ag_r.at[s, 1, 0], down)

    def ag_step(s, step):
        for d in (0, 1):
            c = z - step if d == 0 else z + step
            part_rows = (0, TOP) if d == 0 else (TOP, ROWS - TOP)
            lo, size = part_rows if step == 4 else (0, ROWS)
            spot = full.at[s, block(c, lo, size)]
            remote(spot, spot, ag_s.at[s, d, step - 1], ag_r.at[s, d, step - 1],
                   up if d == 0 else down).wait_recv()
            if step < 4:
                lo, size = part_rows if step == 3 else (0, ROWS)
                spot = full.at[s, block(c, lo, size)]
                go(spot, spot, ag_s.at[s, d, step], ag_r.at[s, d, step], up if d == 0 else down)

    def rows_of(t, low=0, size=TILE):
        return pl.ds(t * TILE + low, size)

    def own_keys():
        row = lax.broadcasted_iota(jnp.int32, (TILE, TILE), 0)
        return lax.broadcasted_iota(jnp.int32, (TILE, TILE), 1) <= row

    def head_columns(h):
        return pl.ds(pl.multiple_of(h * ATT_HD, ATT_HD), ATT_HD)

    def weights_of(t, begin=0, end=HD // ATT_HD):
        rows, low, high = rows_of(t), t * TILE, (t + 1) * TILE

        @pl.loop(begin, end)
        def _(h):
            cols = head_columns(h)
            first = jnp.where(ctx == 0, -1e30, 0.0).astype(F32)
            own = dot(q[rows, cols], k[pl.ds(0, high), cols], 1, 1)
            old = dot(q[rows, cols], kh[pl.ds(low, TOK - low), cols], 1, 1) + first
            blocks = [own[:, :low]] if t else []
            blocks.append(jnp.where(own_keys(), own[:, low:], old[:, :TILE]))
            if high < TOK:
                blocks.append(old[:, TILE:])
            scores = jnp.concatenate(blocks, axis=1)
            peak = jnp.max(scores, axis=1, keepdims=True)
            w = jnp.exp2((scores - peak) * EXP_SCALE)
            total = jnp.sum(w, axis=1, keepdims=True)
            pbuf[h, rows, :] = (w * (1.0 / total)).astype(BF16)

    def attend(t):
        rows, low, high = rows_of(t), t * TILE, (t + 1) * TILE

        @pl.loop(0, HD // ATT_HD)
        def _(h):
            cols = head_columns(h)
            diagonal = pbuf[h, rows, pl.ds(low, TILE)]
            zero = jnp.zeros_like(diagonal)
            value = dot(jnp.where(own_keys(), diagonal, zero), v[pl.ds(low, TILE), cols])
            value += dot(jnp.where(own_keys(), zero, diagonal), vh[pl.ds(low, TILE), cols])
            if t:
                value += dot(pbuf[h, rows, pl.ds(0, low)], v[pl.ds(0, low), cols])
            if high < TOK:
                value += dot(pbuf[h, rows, pl.ds(high, TOK - high)], vh[pl.ds(high, TOK - high), cols])
            att[rows, cols] = value

    def normalize(s):
        g = full[s].astype(F32)
        size = jnp.sqrt(jnp.sum(jnp.sum(g * g, axis=1, keepdims=True), axis=0, keepdims=True))
        x_it[...] = (g * (1.0 / (size + 1e-06))).astype(BF16)

    def iterate():
        for low in (0, 256, 512):
            high = min(low + 256, HD)
            cols = pl.ds(low, high - low)
            strip = dot(x_it[pl.ds(low, HD - low), :], x_it[cols, :], 1, 1).astype(BF16)
            gram[pl.ds(low, HD - low), cols] = strip
            if high < HD:
                gram[cols, pl.ds(high, HD - high)] = jnp.transpose(strip[high - low:, :])
        prod[...] = dot(gram[...], x_it[...]).astype(BF16)
        second = dot(gram[...], prod[...])
        x_it[...] = (
            quintic_first * x_it[...].astype(F32)
            + quintic_second * prod[...].astype(F32)
            + quintic_third * second
        ).astype(BF16)

    def renew(s):
        initial = (wd, wl, wg)[s][...].astype(F32)
        updated = initial + x_it[...].astype(F32)
        target = jnp.sqrt(jnp.sum(initial * initial, axis=0, keepdims=True))
        current = jnp.sqrt(jnp.sum(updated * updated, axis=0, keepdims=True) + 1e-06)
        ren[s] = (updated * (target / current)).astype(BF16)

    def gradient(s):
        left, right = ((hid, scaled), (k, g_lift), (k, g_gate))[s]
        part[s] = dot(left[...], right[...], 0, 0).astype(BF16)

    gradient(0)
    rs_begin(0)
    gradient(1)
    gradient(2)
    rs_step(0, 1)
    rs_begin(1)
    rs_begin(2)
    rs_step(0, 2)
    rs_step(1, 1)
    rs_step(2, 1)
    halo_climb(0)
    rs_step(0, 3)
    rs_step(1, 2)
    rs_step(2, 2)
    halo_land(0)
    rs_end(0)
    rs_step(1, 3)
    rs_step(2, 3)
    rs_end(1)
    halo_wait(0)
    weights_of(0, 0, 3)
    ag_begin(0)
    weights_of(0, 3, 5)
    rs_end(2)
    halo_begin(1)
    halo_half(1, 0)
    halo_half(1, 1)
    for h in range(2 * NX):
        go(weight.at[h], wbuf.at[h], wx_s.at[h], wx_r.at[h], partner)
    for load in loads:
        load.start()
    weights_of(1, 0, 3)
    ag_step(0, 1)
    weights_of(1, 3, 5)
    ag_begin(1)
    weights_of(2, 0, 3)
    ag_step(0, 2)
    halo_climb(1)
    weights_of(2, 3, 5)
    ag_begin(2)
    weights_of(3, 0, 3)
    ag_step(1, 1)
    weights_of(3, 3, 5)
    ag_step(0, 3)
    ag_step(2, 1)
    ag_step(1, 2)
    ag_step(0, 4)
    normalize(0)
    iterate()
    ag_step(2, 2)
    iterate()
    ag_step(1, 3)
    halo_land(1)
    iterate()
    ag_step(2, 3)
    renew(0)
    ag_step(1, 4)
    normalize(1)
    iterate()
    ag_step(2, 4)
    iterate()
    iterate()
    renew(1)
    normalize(2)
    iterate()
    iterate()
    iterate()
    renew(2)
    halo_wait(1)

    chunks = TOK // TILE
    half = TILE // 2
    for t in (0, 2, 1, 3):
        attend(t)
        rows = rows_of(t)
        gate = dot(q[rows, :], ren[2])
        lift = dot(q[rows, :], ren[1])
        applied = (gate * logistic(gate) * lift).astype(BF16)
        result = dot(applied, ren[0])
        back = lax.rsqrt(jnp.mean(result * result, axis=1, keepdims=True) + 1e-06)
        cbuf[head, rows, :] = (att[rows, :] + result * back * gain[...][None, :]).astype(BF16)
        spot = cbuf.at[head, rows]
        side, c = t // 2, t % 2
        go(spot, spot, d1_s.at[0, t], d1_r.at[0, core, c], {"head": chip(1) * 2 + side})
        go(spot, spot, d1_s.at[1, t], d1_r.at[1, core, c], {"head": chip(-1) * 2 + side})

        @pl.when(core != side)
        def _():
            remote(spot, spot, pr_s.at[c], pr_r.at[c], partner).start()

    def here(c, low=0, size=TILE):
        return pl.ds(pl.multiple_of(core * 2 * TILE + c * TILE + low, half), size)

    def near(c):
        for p in (0, 1):
            for d in (0, 1):
                h = chip(2 * d - 1) * 2 + p
                spot = cbuf.at[h, here(c)]
                arrived(spot, d1_s.at[d, 0], d1_r.at[d, p, c], left if d == 0 else right)
                piece = cbuf.at[h, here(c, d * half, half)]
                go(piece, piece, d2_s.at[d, p, c], d2_r.at[d, p, c], right if d == 0 else left)

    def far(p, c):
        for d in (0, 1):
            piece = cbuf.at[chip(2) * 2 + p, here(c, d * half, half)]
            arrived(piece, d2_s.at[d, p, c], d2_r.at[d, p, c], left if d == 0 else right)

    def mirrored(c):
        spot = cbuf.at[place(0, 1), here(c)]
        arrived(spot, pr_s.at[c], pr_r.at[c], partner)

    def add(i, c=None, first=False, last=False):
        h = order[i]
        rows = pl.ds(core * 2 * TILE, 2 * TILE) if c is None else here(c)
        spot = pl.ds(0, 2 * TILE) if c is None else pl.ds(c * TILE, TILE)
        tokens = cbuf[h, rows, :]
        for matrix, total, result in ((wbuf, acc_other, o_out), (wown, acc, None)):
            value = dot(tokens, matrix[h])
            if not first:
                value += total[spot, :]
            if not last:
                total[spot, :] = value
            elif result is None:
                out[rows, :] = value.astype(BF16)
            else:
                result[spot, :] = value.astype(BF16)
                go(o_out.at[spot], o_in.at[spot], o_s.at[c], o_r.at[c], partner)

    def weights_here(i):
        h = order[i]
        loads[i].wait()
        arrived(wbuf.at[h], wx_s.at[h], wx_r.at[h], partner)

    for i in range(2 * NX):
        weights_here(i)
    near(0)
    add(0, first=True)
    for c in (0, 1):
        mirrored(c)
    add(1)
    near(1)
    for i in (2, 3, 4, 5):
        add(i)
    for c in (0, 1):
        for p in (0, 1):
            far(p, c)
            add(6 + p, c, last=p == 1)
    other = pl.ds(pl.multiple_of((1 - core) * 2 * TILE, 2 * TILE), 2 * TILE)
    for c in (0, 1):
        spot = o_in.at[pl.ds(c * TILE, TILE)]
        arrived(spot, o_s.at[c], o_r.at[c], partner)
    out[other, :] = o_in[...]
    for copy in started:
        copy.wait_send()
    for c in (0, 1):
        spot = cbuf.at[head, rows_of(c)]
        remote(spot, spot, pr_s.at[c], pr_r.at[c], partner).wait_send()
    halo_sent(0)
    halo_sent(1)


def layer(queries, key_rows, value_rows, rates, fast_gate, fast_lift, fast_down, gain, weight):
    vmem = pl.BlockSpec(memory_space=pltpu.VMEM)
    dma = pltpu.SemaphoreType.DMA
    square = (HD, HD)
    tokens = (TOK, HD)
    heads = 2 * NX
    chunks = TOK // TILE
    return pl.pallas_call(
        layer_kernel,
        name="layer",
        out_shape=jax.ShapeDtypeStruct(tokens, BF16),
        in_specs=[vmem] * 8 + [pl.BlockSpec(memory_space=pl.ANY)],
        out_specs=vmem,
        scratch_shapes=[
            pltpu.VMEM((3, HD, HD), BF16),
            pltpu.VMEM((3, 2, 4, ROWS, HD), BF16),
            pltpu.VMEM((3, NY, ROWS, HD), BF16),
            pltpu.VMEM((3, HD, HD), BF16),
            pltpu.VMEM(tokens, BF16),
            pltpu.VMEM(tokens, BF16),
            pltpu.VMEM((2, 2, TILE, HD), BF16),
            pltpu.VMEM((HD // ATT_HD, TOK, TOK), BF16),
            pltpu.VMEM(tokens, BF16),
            pltpu.VMEM(tokens, BF16),
            pltpu.VMEM(tokens, BF16),
            pltpu.VMEM(tokens, BF16),
            pltpu.VMEM(square, BF16),
            pltpu.VMEM(square, BF16),
            pltpu.VMEM(square, BF16),
            pltpu.VMEM((TOK, TILE), F32),
            pltpu.VMEM(tokens, F32),
            pltpu.VMEM((3, HD, HD), BF16),
            pltpu.VMEM((heads, TOK, HD), BF16),
            pltpu.VMEM((heads, HD, HD), BF16),
            pltpu.VMEM((heads, HD, HD), BF16),
            pltpu.VMEM((TOK // 2, HD), F32),
            pltpu.VMEM((TOK // 2, HD), F32),
            pltpu.VMEM((TOK // 2, HD), BF16),
            pltpu.VMEM((TOK // 2, HD), BF16),
            dma((2, 2)), dma((2,)),
            dma((2, 5)), dma((2, 2)),
            dma((3, 2, 4)), dma((3, 2, 4)),
            dma((3, 3)), dma((3, 3)),
            dma((3, 2, 4)), dma((3, 2, 4)),
            dma((heads,)),
            dma((heads,)), dma((heads,)),
            dma((2, chunks)), dma((2, 2, 2)),
            dma((2, 2, 2)), dma((2, 2, 2)),
            dma((2,)), dma((2,)),
            dma((2,)), dma((2,)),
        ],
        compiler_params=pltpu.CompilerParams(
            collective_id=0, has_side_effects=True, vmem_limit_bytes=60 * 1024 * 1024
        ),
    )(queries, key_rows, value_rows, rates, fast_gate, fast_lift, fast_down, gain, weight)


def on_device(
    queries, key_rows, value_rows, learning_rates, fast_gate, fast_lift, fast_down, output_gain, output_weight
):
    return layer(
        queries, key_rows, value_rows, learning_rates, fast_gate[0], fast_lift[0], fast_down[0],
        output_gain, output_weight.reshape(2 * NX, HD, HD),
    )


def solution(mesh):
    return jax.shard_map(
        on_device,
        mesh=mesh,
        in_specs=(
            P("ctx", "head"),
            P("ctx", "head"),
            P("ctx", "head"),
            P("head", "ctx"),
            P("head", None, None),
            P("head", None, None),
            P("head", None, None),
            P("head"),
            P(None, "head"),
        ),
        out_specs=P("ctx", "head"),
        check_vma=False,
    )
```
